32 devices in a mesh: seq: 8 (over y, x, core), tp: 4 (over z).
Axes of the slice: x: 2, y: 2, z: 4, core: 2. Of those that a mesh axis runs over, the one named last changes fastest.
Arguments:
- queries: bfloat16 [384, 2048], P('seq', 'tp'), may hold values from -16 to 16
- keys: bfloat16 [384, 2048], P('seq', 'tp'), may hold values from -16 to 16
- values: bfloat16 [384, 2048], P('seq', 'tp'), may hold values from -6 to 6
- patch_stream: bfloat16 [384, 4096], P('seq', 'tp'), may hold values from -6 to 6
- out_weight: bfloat16 [2048, 4096], P('tp', 'seq'), may hold values from -1 to 1
- down_weight: bfloat16 [4096, 1280], P('tp'), may hold values from -0.09375 to 0.09375
- byte_states: bfloat16 [1536, 1280], P('seq', 'tp'), may hold values from -6 to 6
- patch_starts: int32 [8, 48], P('seq'), may hold values from 0 to 192, as said below
Outputs:
- new_patches: bfloat16 [384, 4096], P('seq', 'tp')
- new_bytes: bfloat16 [1536, 1280], P('seq', 'tp')
The draws below stay inside these ranges and needn't reach their ends.
Inputs may be any that keep to these rules, and one draw needn't show every extreme that they name: `patch_starts`: each row d lists rising offsets within device d's 192 bytes at which patches start: the first is 0 in row 0 and from 4 to 7 in the other rows, the others are 8 or more; at least 24 entries of a row are offsets, some row has all 48, and the remaining entries at the end of a row equal 192.
All inputs are finite; a program needn't handle non-finite values.
Results may differ from the reference program's by a relative error of at most 0.015.
Values may be sent and summed in bfloat16 or wider, within the bound.
A program may use at most 128 MiB of HBM per device.

```python
import jax
import jax.numpy as jnp
from jax import lax

D = 4096
DL = 1280
HEADS = 16
DH = 128
B_DEV = 192
EDGE = 8
P_CAP = 48
HW = 2048
PATCHES = 384
BYTES = 1536
N_SEQ = 8


def drawn_rows(key, salt):
    return jnp.clip(jax.random.normal(jax.random.fold_in(key, salt), (PATCHES, HW), jnp.float32), -6.0, 6.0)


def draw_queries(key, part):
    rows = drawn_rows(key, 1)
    return rows.astype(jnp.bfloat16)


def draw_keys(key, part):
    rows = drawn_rows(key, 2)
    return rows.astype(jnp.bfloat16)


def draw_patch_starts(key, part):
    inner = jax.random.fold_in(key, 11)
    count_key, first_key, pick_key, full_key, edge_key = jax.random.split(inner, 5)
    device = jnp.arange(N_SEQ, dtype=jnp.int32)
    counts = jax.random.randint(count_key, (N_SEQ,), P_CAP // 2, P_CAP + 1)
    full_device = jax.random.randint(full_key, (), 0, N_SEQ)
    counts = jnp.where(device == full_device, P_CAP, counts)
    firsts = jax.random.randint(first_key, (N_SEQ,), EDGE // 2, EDGE)
    edge_device = jax.random.randint(edge_key, (), 1, N_SEQ)
    firsts = jnp.where(device == edge_device, EDGE - 1, firsts)
    firsts = jnp.where(device == 0, 0, firsts)

    def one_row(row_key, count, first):
        order = jax.random.permutation(row_key, B_DEV - EDGE)[:P_CAP - 1] + EDGE
        place = jnp.arange(P_CAP - 1, dtype=jnp.int32)
        rest = jnp.where(place < count - 1, order, B_DEV)
        rest = jnp.sort(rest)
        return jnp.concatenate([first[None], rest]).astype(jnp.int32)
    row_keys = jax.random.split(pick_key, N_SEQ)
    return jax.vmap(one_row)(row_keys, counts, firsts)


def levels(rng, dims, cuts, least, largest):
    factor_of = 1.0
    for dim, parts in cuts:
        draws = jax.random.uniform(jax.random.fold_in(jax.random.fold_in(rng, 6), dim), (parts,), jnp.float32, least / len(cuts), largest / len(cuts))
        factor_of = factor_of * jnp.repeat(jnp.exp(draws), dims[dim] // parts).reshape((-1,) + (1,) * (len(dims) - 1 - dim))
    return factor_of


def gaussian(rng, shape, width, bound, cuts=(), kind=jnp.bfloat16):
    level = levels(rng, shape, cuts, -0.22, 0.18) if cuts else 1.0
    array = jax.random.normal(rng, shape, jnp.float32) * width * level
    return jnp.minimum(jnp.maximum(array, -bound), bound).astype(kind)


def setup_inputs(seed: int = 0) -> dict:
    streams_of = jax.random.split(jax.random.key(seed), 9)
    queries = draw_queries(jax.random.fold_in(streams_of[8], 71), 0)
    keys = draw_keys(jax.random.fold_in(streams_of[8], 71), 0)
    values = gaussian(streams_of[2], (PATCHES, HW), 1.0, 6.0, ((0, 8), (1, 4)))
    patch_stream = gaussian(streams_of[3], (PATCHES, D), 1.0, 6.0, ((0, 8), (1, 4)))
    out_weight = gaussian(streams_of[4], (HW, D), (HW // 64) ** -0.5, 1.0, ((0, 4), (1, 8)))
    down_weight = gaussian(streams_of[5], (D, DL), D ** -0.5, 0.09375, ((0, 4),))
    byte_states = gaussian(streams_of[6], (BYTES, DL), 1.0, 6.0, ((0, 8), (1, 4)))
    patch_starts = draw_patch_starts(jax.random.fold_in(streams_of[8], 71), 0)
    return dict(queries=queries, keys=keys, values=values, patch_stream=patch_stream, out_weight=out_weight, down_weight=down_weight, byte_states=byte_states, patch_starts=patch_starts)


NEG = -1.0e30


def reference(queries, keys, values, patch_stream, out_weight, down_weight, byte_states, patch_starts):
    total_slots = queries.shape[0]
    valid = (patch_starts.reshape(-1) < B_DEV)
    slot_ids = jnp.arange(total_slots, dtype=jnp.int32)
    key_heads = keys.reshape(total_slots, HEADS, DH).astype(jnp.float32)
    value_heads = values.reshape(total_slots, HEADS, DH).astype(jnp.float32)
    block_rows = 256 if total_slots % 256 == 0 else P_CAP
    scale = DH ** -0.5

    def one_block(index):
        begin = (index * block_rows).astype(jnp.int32)
        query_block = lax.dynamic_slice_in_dim(queries, begin, block_rows, 0)
        query_heads = query_block.reshape(block_rows, HEADS, DH).astype(jnp.float32)
        scores = jnp.einsum("qhd,khd->hqk", query_heads, key_heads) * scale
        query_ids = begin + jnp.arange(block_rows, dtype=jnp.int32)
        allowed = valid[None, :] & (slot_ids[None, :] <= query_ids[:, None])
        scores = jnp.where(allowed[None], scores, NEG)
        peak = jnp.max(scores, axis=-1, keepdims=True)
        expo = jnp.where(allowed[None], jnp.exp(scores - peak), 0.0)
        total = jnp.sum(expo, axis=-1)
        weights = expo.astype(jnp.bfloat16).astype(jnp.float32)
        summed = jnp.einsum("hqk,khd->qhd", weights, value_heads)
        result = summed / jnp.transpose(total)[:, :, None]
        return result.reshape(block_rows, HEADS * DH).astype(jnp.bfloat16)

    attn = lax.map(one_block, jnp.arange(total_slots // block_rows, dtype=jnp.int32))
    attn = attn.reshape(total_slots, HEADS * DH)
    mixed = jnp.dot(attn, out_weight, preferred_element_type=jnp.float32)
    new_patches = (patch_stream.astype(jnp.float32) + mixed).astype(jnp.bfloat16)
    patch_down = jnp.dot(new_patches, down_weight, preferred_element_type=jnp.float32).astype(jnp.bfloat16)

    valid_rows = patch_starts < B_DEV
    counts = jnp.sum(valid_rows.astype(jnp.int32), axis=1)
    position = jnp.arange(B_DEV, dtype=jnp.int32)
    below = jnp.sum((patch_starts[:, None, :] <= position[None, :, None]).astype(jnp.int32), axis=2)
    device = jnp.arange(patch_starts.shape[0], dtype=jnp.int32)[:, None]
    prev_slot = (device - 1) * P_CAP + jnp.roll(counts, 1)[:, None] - 1
    owner = jnp.where(below > 0, device * P_CAP + below - 1, prev_slot)
    owner = jnp.maximum(owner, 0).astype(jnp.int32)
    gathered = jnp.take(patch_down, owner.reshape(-1), axis=0)
    new_bytes = (byte_states.astype(jnp.float32) + gathered.astype(jnp.float32)).astype(jnp.bfloat16)
    return new_patches, new_bytes
```

```python
import functools

import jax
import jax.numpy as jnp
from jax import lax
from jax.experimental import pallas as pl
from jax.experimental.pallas import tpu as pltpu
from jax.sharding import PartitionSpec as P

DH = 128
B_DEV = 192


NEG = -1e30


def from_behind(value, axis, by):
    devices = lax.axis_size(axis)
    pairs = [(i, i + by) for i in range(devices) if 0 <= i + by < devices]
    return lax.ppermute(value, axis, pairs)


def plain_form(
    queries, keys, values, patch_stream, out_weight, down_weight, byte_states, patch_starts
):
    rows = queries.shape[0]
    width = queries.shape[1]
    heads = width // DH
    scale = DH ** (-0.5)
    starts_row = patch_starts.reshape(-1)
    valid = starts_row < B_DEV
    key_mask = valid.astype(jnp.bfloat16)
    first_slot = lax.axis_index("seq") * rows
    query_ids = first_slot + jnp.arange(rows, dtype=jnp.int32)
    query_heads = queries.reshape(rows, heads, DH)
    peak = jnp.full((heads, rows), NEG, jnp.float32)
    key_piece = lax.all_gather(keys, "seq", axis=0, tiled=True)
    value_piece = lax.all_gather(values, "seq", axis=0, tiled=True)
    mask_piece = lax.all_gather(key_mask, "seq", axis=0, tiled=True)
    count = key_piece.shape[0]
    key_heads = key_piece.reshape(count, heads, DH)
    value_heads = value_piece.reshape(count, heads, DH)
    scores = (
        jnp.einsum("qhd,khd->hqk", query_heads, key_heads, preferred_element_type=jnp.float32)
        * scale
    )
    key_ids = jnp.arange(count, dtype=jnp.int32)
    allowed = (mask_piece > 0)[None, :] & (key_ids[None, :] <= query_ids[:, None])
    scores = jnp.where(allowed[None], scores, NEG)
    new_peak = jnp.maximum(peak, jnp.max(scores, axis=-1))
    expo = jnp.exp(scores - new_peak[:, :, None])
    total = jnp.sum(expo, axis=-1)
    weights = expo.astype(jnp.bfloat16)
    summed = jnp.einsum("hqk,khd->hqd", weights, value_heads, preferred_element_type=jnp.float32)
    peak, total, summed = (new_peak, total, summed)
    attn = summed / total[:, :, None]
    attn = jnp.transpose(attn, (1, 0, 2)).reshape(rows, width).astype(jnp.bfloat16)
    partial_value = jnp.dot(
        attn,
        lax.all_gather(out_weight, "seq", axis=1, tiled=True),
        preferred_element_type=jnp.float32,
    )
    mixed = lax.psum_scatter(
        partial_value.astype(jnp.bfloat16), "tp", scatter_dimension=1, tiled=True
    ).astype(jnp.float32)
    new_patches = (patch_stream.astype(jnp.float32) + mixed).astype(jnp.bfloat16)
    down_terms = jnp.dot(new_patches, down_weight, preferred_element_type=jnp.float32)
    patch_down = lax.psum_scatter(
        down_terms.astype(jnp.bfloat16), "tp", scatter_dimension=1, tiled=True
    )
    following = jnp.concatenate([valid[1:], jnp.zeros((1,), jnp.bool_)])
    last_pick = (valid & jnp.logical_not(following)).astype(jnp.bfloat16)[None, :]
    last_state = jnp.dot(last_pick, patch_down, preferred_element_type=jnp.float32).astype(
        jnp.bfloat16
    )
    earlier_state = from_behind(last_state, "seq", 1)
    position = jnp.arange(B_DEV, dtype=jnp.int32)
    ends = jnp.concatenate([starts_row[1:], jnp.full((1,), B_DEV, jnp.int32)])
    member = (starts_row[None, :] <= position[:, None]) & (position[:, None] < ends[None, :])
    member = member.astype(jnp.bfloat16)
    before = (position < starts_row[0]).astype(jnp.float32)[:, None]
    added = jnp.dot(member, patch_down, preferred_element_type=jnp.float32)
    added = added + before * earlier_state.astype(jnp.float32)
    new_bytes = (byte_states.astype(jnp.float32) + added).astype(jnp.bfloat16)
    return (new_patches, new_bytes)


MESH = pl.DeviceIdType.MESH


def fused_kernel(
    sizes,
    q_hbm, k_hbm, v_hbm, ps_hbm, ow_hbm, dw_hbm, bs_hbm, st_ref,
    np_hbm, nb_hbm,
    qbuf, kbuf, vbuf, sbuf, aown, abuf, cbuf, rbuf, npbuf, dsend, dbuf, lsend, lbuf,
    ow, dw, ps, bs, pd, nb,
    qs, qr, ks, kr, vs, vr, ss, sr, as_, ar, cs, cr, ds_, dr, ls, lr, loc,
):
    S, T, H, rows, local = sizes
    G = S // H
    CP = S // T
    cols = ow.shape[1]
    me = lax.axis_index("seq")
    z = lax.axis_index("tp")
    head = me // G
    g = lax.rem(me, G)

    loads = [
        pltpu.make_async_copy(src, dst, loc.at[n])
        for n, (src, dst) in enumerate(
            ((ow_hbm, ow), (ps_hbm, ps), (dw_hbm, dw), (bs_hbm, bs))
        )
    ]
    for load in loads:
        load.start()

    starts = jnp.broadcast_to(st_ref[...], (8, rows))
    valid8 = jnp.where(starts < B_DEV, 1.0, 0.0)
    sbuf[me] = valid8

    barrier = pltpu.get_barrier_semaphore()
    for i in range(S):
        for t in range(T):
            if i or t:
                pl.semaphore_signal(
                    barrier, inc=1,
                    device_id={"seq": lax.rem(me + i, S), "tp": lax.rem(z + t, T)},
                    device_id_type=MESH,
                )
    pl.semaphore_wait(barrier, S * T - 1)

    def lanes(block, width):
        return pl.ds(pl.multiple_of(block * width, 128), width)

    sends = []

    def send(src, dst, ssem, rsem, seq, tp):
        copy = pltpu.make_async_remote_copy(
            src_ref=src, dst_ref=dst, send_sem=ssem, recv_sem=rsem,
            device_id={"seq": seq, "tp": tp}, device_id_type=MESH,
        )
        copy.start()
        sends.append(copy)

    def arrived(dst, sem):
        pltpu.make_async_copy(dst, dst, sem).wait()

    for i in range(S):
        tgt = lax.rem(me + i, S)
        part = lanes(tgt // G, DH)
        if i == 0:
            pltpu.make_async_copy(k_hbm.at[:, part], kbuf.at[me], kr.at[me]).start()
            pltpu.make_async_copy(v_hbm.at[:, part], vbuf.at[me], vr.at[me]).start()
            pltpu.make_async_copy(q_hbm.at[:, part], qbuf.at[head], qr.at[head]).start()
        else:
            send(k_hbm.at[:, part], kbuf.at[me], ks.at[i], kr.at[me], tgt, z)
            if i % G == 0:
                send(q_hbm.at[:, part], qbuf.at[head], qs.at[i], qr.at[head], tgt, z)
            send(sbuf.at[me], sbuf.at[me], ss.at[i], sr.at[me], tgt, z)
            send(v_hbm.at[:, part], vbuf.at[me], vs.at[i], vr.at[me], tgt, z)

    count = S * rows
    key_row = lax.broadcasted_iota(jnp.int32, (rows, count), 1)
    slot = lax.broadcasted_iota(jnp.int32, (rows, count), 0)
    spread = key_row == slot
    for d in range(1, S):
        spread = spread | (key_row == slot + d * rows)
    spread = jnp.where(spread, 1.0, 0.0).astype(jnp.bfloat16)

    for i in range(1, S):
        src = lax.rem(me + i, S)
        arrived(sbuf.at[src], sr.at[src])
    which = lax.broadcasted_iota(jnp.int32, (S, rows), 0)
    valid = jnp.zeros((S, rows), jnp.float32)
    for d in range(S):
        valid = jnp.where(which == d, sbuf[d][:1, :], valid)
    laid = jnp.dot(valid.astype(jnp.bfloat16), spread, preferred_element_type=jnp.float32)
    owner = lax.broadcasted_iota(jnp.int32, (S, count), 0) * rows
    lane = lax.broadcasted_iota(jnp.int32, (S, count), 1)
    laid = jnp.where((lane >= owner) & (lane < owner + rows), laid, 0.0)
    key_valid = jnp.sum(laid, axis=0, keepdims=True)

    mine = H * rows
    row = lax.broadcasted_iota(jnp.int32, (mine, count), 0)
    block = jnp.zeros((mine, count), jnp.int32)
    for j in range(1, H):
        block = block + jnp.where(row >= j * rows, (G - 1) * rows, 0)
    query = row + block + g * rows
    key = lax.broadcasted_iota(jnp.int32, (mine, count), 1)
    allowed = (key <= query) & (key_valid > 0.0)

    for j in range(H):
        arrived(qbuf.at[j], qr.at[j])
    for d in range(S):
        arrived(kbuf.at[d], kr.at[d])
    scores = lax.dot_general(
        qbuf[...].reshape(mine, DH), kbuf[...].reshape(count, DH),
        (((1,), (1,)), ((), ())), preferred_element_type=jnp.float32,
    ) * (DH ** -0.5)
    scores = jnp.where(allowed, scores, NEG)
    peak = jnp.max(scores, axis=1, keepdims=True)
    expo = jnp.exp(scores - peak)
    total = jnp.sum(expo, axis=1, keepdims=True)
    for d in range(S):
        arrived(vbuf.at[d], vr.at[d])
    summed = jnp.dot(
        expo.astype(jnp.bfloat16), vbuf[...].reshape(count, DH),
        preferred_element_type=jnp.float32,
    )
    aown[...] = (summed / total).astype(jnp.bfloat16).reshape(H, rows, DH)

    for e in range(G):
        for jj in range(H):
            i = jj * G + e
            tgt = lax.rem(me + i, S)
            dst = abuf.at[g, :, :, lanes(head, DH)]
            if i == 0:
                pltpu.make_async_copy(aown, dst, ar.at[me]).start()
            else:
                send(aown, dst, as_.at[i], ar.at[me], tgt, z)
    loads[0].wait()

    chunk = me // CP
    place = lax.rem(me, CP)
    for e in range(G):
        gg = lax.rem(g + e, G)
        for jj in range(H):
            src = lax.rem(head + jj, H) * G + gg
            arrived(aown, ar.at[src])
        product = jnp.dot(
            abuf[gg].reshape(mine, H * DH), ow[...], preferred_element_type=jnp.float32
        )
        cbuf[gg] = product.astype(jnp.bfloat16).reshape(H, rows, cols)
        for jj in range(H):
            j = lax.rem(head + jj, H)
            tgt = j * G + gg
            n = e * H + jj
            out = pltpu.make_async_remote_copy(
                src_ref=cbuf.at[gg, j], dst_ref=rbuf.at[z, place],
                send_sem=cs.at[n], recv_sem=cr.at[z, place],
                device_id={"seq": tgt, "tp": chunk}, device_id_type=MESH,
            )
            if n == 0:
                home = chunk == z

                @pl.when(home)
                def _():
                    pltpu.make_async_copy(
                        cbuf.at[gg, j], rbuf.at[z, place], cr.at[z, place]
                    ).start()

                @pl.when(jnp.logical_not(home))
                def _():
                    out.start()

                first_out = out
            else:
                out.start()
                sends.append(out)

    loads[1].wait()
    for t in range(T):
        for p in range(CP):
            arrived(rbuf.at[t, p], cr.at[t, p])
    for p in range(CP):
        mixed = rbuf[0, p].astype(jnp.float32)
        for t in range(1, T):
            mixed = mixed + rbuf[t, p].astype(jnp.float32)
        at = pl.ds(p * cols, cols)
        npbuf[:, at] = (ps[:, at].astype(jnp.float32) + mixed).astype(jnp.bfloat16)
    np_out = pltpu.make_async_copy(npbuf, np_hbm, loc.at[4])
    np_out.start()

    loads[2].wait()
    wide = dw.shape[1]
    padded = dbuf.shape[2]
    down = jnp.dot(npbuf[...], dw[...], preferred_element_type=jnp.float32)

    def share(x, t):
        turned = x if t == 0 else pltpu.roll(x, wide - t * local, 1)
        return turned[:, :padded].astype(jnp.bfloat16)

    for t in range(T):
        dsend[t] = share(down, t)
    for i in range(1, T):
        t = lax.rem(z + i, T)
        send(dsend.at[t], dbuf.at[z], ds_.at[i], dr.at[z], me, t)
    dbuf[z] = dsend[z]

    held = jnp.sum(valid8[:1, :], axis=1, keepdims=True)
    lane16 = lax.broadcasted_iota(jnp.int32, (16, rows), 1).astype(jnp.float32)
    pick = jnp.where(lane16 == held - 1.0, 1.0, 0.0).astype(jnp.bfloat16)
    last = jnp.dot(pick, down.astype(jnp.bfloat16), preferred_element_type=jnp.float32)
    for t in range(T):
        lsend[t] = share(last, t)
    after = lax.rem(me + 1, S)
    for i in range(T):
        t = lax.rem(z + i, T)
        send(lsend.at[t], lbuf.at[z], ls.at[i], lr.at[z], after, t)

    position = lax.broadcasted_iota(jnp.int32, (B_DEV, rows), 0)
    begun = jnp.where(st_ref[...] <= position, 1.0, 0.0)
    reached = jnp.sum(begun, axis=1, keepdims=True)
    lane_b = lax.broadcasted_iota(jnp.int32, (B_DEV, rows), 1).astype(jnp.float32)
    member = jnp.where(lane_b == reached - 1.0, 1.0, 0.0).astype(jnp.bfloat16)
    before = reached < 0.5
    loads[3].wait()

    for i in range(1, T):
        t = lax.rem(z + i, T)
        arrived(dbuf.at[t], dr.at[t])
    for t in range(T):
        arrived(lbuf.at[t], lr.at[t])
    state = dbuf[0].astype(jnp.float32)
    earlier = lbuf[0].astype(jnp.float32)
    for t in range(1, T):
        state = state + dbuf[t].astype(jnp.float32)
        earlier = earlier + lbuf[t].astype(jnp.float32)
    state = state.astype(jnp.bfloat16)
    earlier = earlier.astype(jnp.bfloat16).astype(jnp.float32)[:1, :]
    added = jnp.dot(member, state, preferred_element_type=jnp.float32)
    pd[...] = jnp.where(before, earlier, added)
    nb[...] = (bs[...].astype(jnp.float32) + pd[:, :local]).astype(jnp.bfloat16)
    nb_out = pltpu.make_async_copy(nb, nb_hbm, loc.at[5])
    nb_out.start()

    for copy in sends:
        copy.wait_send()

    @pl.when(jnp.logical_not(home))
    def _():
        first_out.wait_send()

    np_out.wait()
    nb_out.wait()


def fused_form(
    S, T, queries, keys, values, patch_stream, out_weight, down_weight, byte_states, patch_starts
):
    rows, width = queries.shape
    H = width // DH
    G = S // H
    cols = out_weight.shape[1]
    bytes_here, local = byte_states.shape
    padded = -(-local // 128) * 128
    bf = jnp.bfloat16
    sem = pltpu.SemaphoreType.DMA
    scratch = [
        pltpu.VMEM((H, rows, DH), bf),
        pltpu.VMEM((S, rows, DH), bf),
        pltpu.VMEM((S, rows, DH), bf),
        pltpu.VMEM((S, 8, rows), jnp.float32),
        pltpu.VMEM((H, rows, DH), bf),
        pltpu.VMEM((G, H, rows, width), bf),
        pltpu.VMEM((G, H, rows, cols), bf),
        pltpu.VMEM((T, S // T, rows, cols), bf),
        pltpu.VMEM(patch_stream.shape, bf),
        pltpu.VMEM((T, rows, padded), bf),
        pltpu.VMEM((T, rows, padded), bf),
        pltpu.VMEM((T, 16, padded), bf),
        pltpu.VMEM((T, 16, padded), bf),
        pltpu.VMEM(out_weight.shape, bf),
        pltpu.VMEM(down_weight.shape, bf),
        pltpu.VMEM(patch_stream.shape, bf),
        pltpu.VMEM(byte_states.shape, bf),
        pltpu.VMEM((bytes_here, padded), jnp.float32),
        pltpu.VMEM(byte_states.shape, bf),
        sem((S,)), sem((H,)), sem((S,)), sem((S,)), sem((S,)), sem((S,)),
        sem((S,)), sem((S,)), sem((S,)), sem((S,)), sem((S,)), sem((T, S // T)),
        sem((T,)), sem((T,)), sem((T,)), sem((T,)), sem((6,)),
    ]
    hbm = pl.BlockSpec(memory_space=pl.ANY)
    return tuple(pl.pallas_call(
        functools.partial(fused_kernel, (S, T, H, rows, local)),
        out_shape=(
            jax.ShapeDtypeStruct(patch_stream.shape, bf),
            jax.ShapeDtypeStruct(byte_states.shape, bf),
        ),
        in_specs=[hbm] * 7 + [pl.BlockSpec(memory_space=pltpu.VMEM)],
        out_specs=(hbm, hbm),
        scratch_shapes=scratch,
        compiler_params=pltpu.CompilerParams(collective_id=0, has_side_effects=True),
    )(queries, keys, values, patch_stream, out_weight, down_weight, byte_states, patch_starts))


def on_device(S, T, *args):
    queries, out_weight = args[0], args[4]
    heads = queries.shape[1] // DH
    aligned = out_weight.shape[1] % 128 == 0 and queries.shape[0] % 16 == 0
    if aligned and S % heads == 0 and S % T == 0 and S >= T:
        return fused_form(S, T, *args)
    return plain_form(*args)


def solution(mesh):
    in_specs = (
        P("seq", "tp"),
        P("seq", "tp"),
        P("seq", "tp"),
        P("seq", "tp"),
        P("tp", "seq"),
        P("tp", None),
        P("seq", "tp"),
        P("seq", None),
    )
    out_specs = (P("seq", "tp"), P("seq", "tp"))
    return jax.shard_map(
        functools.partial(on_device, mesh.shape["seq"], mesh.shape["tp"]),
        mesh=mesh, in_specs=in_specs, out_specs=out_specs, check_vma=False
    )
```

```python
import functools

import jax
import jax.numpy as jnp
from jax import lax
from jax.experimental import pallas as pl
from jax.experimental.pallas import tpu as pltpu
from jax.sharding import PartitionSpec as P

DH = 128
B_DEV = 192


NEG = -1e30


def from_behind(value, axis, by):
    devices = lax.axis_size(axis)
    pairs = [(i, i + by) for i in range(devices) if 0 <= i + by < devices]
    return lax.ppermute(value, axis, pairs)


def plain_form(
    queries, keys, values, patch_stream, out_weight, down_weight, byte_states, patch_starts
):
    rows = queries.shape[0]
    width = queries.shape[1]
    heads = width // DH
    scale = DH ** (-0.5)
    starts_row = patch_starts.reshape(-1)
    valid = starts_row < B_DEV
    key_mask = valid.astype(jnp.bfloat16)
    first_slot = lax.axis_index("seq") * rows
    query_ids = first_slot + jnp.arange(rows, dtype=jnp.int32)
    query_heads = queries.reshape(rows, heads, DH)
    peak = jnp.full((heads, rows), NEG, jnp.float32)
    key_piece = lax.all_gather(keys, "seq", axis=0, tiled=True)
    value_piece = lax.all_gather(values, "seq", axis=0, tiled=True)
    mask_piece = lax.all_gather(key_mask, "seq", axis=0, tiled=True)
    count = key_piece.shape[0]
    key_heads = key_piece.reshape(count, heads, DH)
    value_heads = value_piece.reshape(count, heads, DH)
    scores = (
        jnp.einsum("qhd,khd->hqk", query_heads, key_heads, preferred_element_type=jnp.float32)
        * scale
    )
    key_ids = jnp.arange(count, dtype=jnp.int32)
    allowed = (mask_piece > 0)[None, :] & (key_ids[None, :] <= query_ids[:, None])
    scores = jnp.where(allowed[None], scores, NEG)
    new_peak = jnp.maximum(peak, jnp.max(scores, axis=-1))
    expo = jnp.exp(scores - new_peak[:, :, None])
    total = jnp.sum(expo, axis=-1)
    weights = expo.astype(jnp.bfloat16)
    summed = jnp.einsum("hqk,khd->hqd", weights, value_heads, preferred_element_type=jnp.float32)
    peak, total, summed = (new_peak, total, summed)
    attn = summed / total[:, :, None]
    attn = jnp.transpose(attn, (1, 0, 2)).reshape(rows, width).astype(jnp.bfloat16)
    partial_value = jnp.dot(
        attn,
        lax.all_gather(out_weight, "seq", axis=1, tiled=True),
        preferred_element_type=jnp.float32,
    )
    mixed = lax.psum_scatter(
        partial_value.astype(jnp.bfloat16), "tp", scatter_dimension=1, tiled=True
    ).astype(jnp.float32)
    new_patches = (patch_stream.astype(jnp.float32) + mixed).astype(jnp.bfloat16)
    down_terms = jnp.dot(new_patches, down_weight, preferred_element_type=jnp.float32)
    patch_down = lax.psum_scatter(
        down_terms.astype(jnp.bfloat16), "tp", scatter_dimension=1, tiled=True
    )
    following = jnp.concatenate([valid[1:], jnp.zeros((1,), jnp.bool_)])
    last_pick = (valid & jnp.logical_not(following)).astype(jnp.bfloat16)[None, :]
    last_state = jnp.dot(last_pick, patch_down, preferred_element_type=jnp.float32).astype(
        jnp.bfloat16
    )
    earlier_state = from_behind(last_state, "seq", 1)
    position = jnp.arange(B_DEV, dtype=jnp.int32)
    ends = jnp.concatenate([starts_row[1:], jnp.full((1,), B_DEV, jnp.int32)])
    member = (starts_row[None, :] <= position[:, None]) & (position[:, None] < ends[None, :])
    member = member.astype(jnp.bfloat16)
    before = (position < starts_row[0]).astype(jnp.float32)[:, None]
    added = jnp.dot(member, patch_down, preferred_element_type=jnp.float32)
    added = added + before * earlier_state.astype(jnp.float32)
    new_bytes = (byte_states.astype(jnp.float32) + added).astype(jnp.bfloat16)
    return (new_patches, new_bytes)


MESH = pl.DeviceIdType.MESH


def fused_kernel(
    sizes,
    q_hbm, k_hbm, v_hbm, ps_hbm, ow_hbm, dw_hbm, bs_hbm, st_ref,
    np_hbm, nb_hbm,
    qbuf, kbuf, vbuf, sbuf, aown, abuf, cbuf, rel, rbuf, npbuf, dsend, dbuf, lsend, lbuf,
    ow, dw, ps, bs, pd, nb,
    qs, qr, ks, kr, vs, vr, ss, sr, as_, ar, cs, relr, fs, cr, ds_, dr, ls, lr, loc,
):
    S, T, H, rows, local = sizes
    G = S // H
    CP = S // T
    cols = ow.shape[1]
    me = lax.axis_index("seq")
    z = lax.axis_index("tp")
    head = me // G
    g = lax.rem(me, G)

    loads = [
        pltpu.make_async_copy(src, dst, loc.at[n])
        for n, (src, dst) in enumerate(
            ((ow_hbm, ow), (ps_hbm, ps), (dw_hbm, dw), (bs_hbm, bs))
        )
    ]
    for load in loads:
        load.start()

    starts = jnp.broadcast_to(st_ref[...], (8, rows))
    valid8 = jnp.where(starts < B_DEV, 1.0, 0.0)
    sbuf[me] = valid8

    barrier = pltpu.get_barrier_semaphore()
    for i in range(1, S):
        pl.semaphore_signal(
            barrier, inc=1, device_id={"seq": lax.rem(me + i, S), "tp": z}, device_id_type=MESH
        )
    for i in range(1, T):
        pl.semaphore_signal(
            barrier, inc=1, device_id={"seq": me, "tp": lax.rem(z + i, T)}, device_id_type=MESH
        )
    pl.semaphore_wait(barrier, S + T - 2)

    def lanes(block, width):
        return pl.ds(pl.multiple_of(block * width, 128), width)

    sends = []

    def send(src, dst, ssem, rsem, seq, tp):
        copy = pltpu.make_async_remote_copy(
            src_ref=src, dst_ref=dst, send_sem=ssem, recv_sem=rsem,
            device_id={"seq": seq, "tp": tp}, device_id_type=MESH,
        )
        copy.start()
        sends.append(copy)

    def arrived(dst, sem):
        pltpu.make_async_copy(dst, dst, sem).wait()

    for i in range(S):
        tgt = lax.rem(me + i, S)
        part = lanes(tgt // G, DH)
        if i == 0:
            pltpu.make_async_copy(k_hbm.at[:, part], kbuf.at[me], kr.at[me]).start()
            pltpu.make_async_copy(v_hbm.at[:, part], vbuf.at[me], vr.at[me]).start()
            pltpu.make_async_copy(q_hbm.at[:, part], qbuf.at[head], qr.at[head]).start()
        else:
            send(k_hbm.at[:, part], kbuf.at[me], ks.at[i], kr.at[me], tgt, z)
            if i % G == 0:
                send(q_hbm.at[:, part], qbuf.at[head], qs.at[i], qr.at[head], tgt, z)
            send(sbuf.at[me], sbuf.at[me], ss.at[i], sr.at[me], tgt, z)
            send(v_hbm.at[:, part], vbuf.at[me], vs.at[i], vr.at[me], tgt, z)

    count = S * rows
    key_row = lax.broadcasted_iota(jnp.int32, (rows, count), 1)
    slot = lax.broadcasted_iota(jnp.int32, (rows, count), 0)
    spread = key_row == slot
    for d in range(1, S):
        spread = spread | (key_row == slot + d * rows)
    spread = jnp.where(spread, 1.0, 0.0).astype(jnp.bfloat16)

    for i in range(1, S):
        src = lax.rem(me + i, S)
        arrived(sbuf.at[src], sr.at[src])
    which = lax.broadcasted_iota(jnp.int32, (S, rows), 0)
    valid = jnp.zeros((S, rows), jnp.float32)
    for d in range(S):
        valid = jnp.where(which == d, sbuf[d][:1, :], valid)
    laid = jnp.dot(valid.astype(jnp.bfloat16), spread, preferred_element_type=jnp.float32)
    owner = lax.broadcasted_iota(jnp.int32, (S, count), 0) * rows
    lane = lax.broadcasted_iota(jnp.int32, (S, count), 1)
    laid = jnp.where((lane >= owner) & (lane < owner + rows), laid, 0.0)
    key_valid = jnp.sum(laid, axis=0, keepdims=True)

    mine = H * rows
    row = lax.broadcasted_iota(jnp.int32, (mine, count), 0)
    block = jnp.zeros((mine, count), jnp.int32)
    for j in range(1, H):
        block = block + jnp.where(row >= j * rows, (G - 1) * rows, 0)
    query = row + block + g * rows
    key = lax.broadcasted_iota(jnp.int32, (mine, count), 1)
    allowed = (key <= query) & (key_valid > 0.0)

    for j in range(H):
        arrived(qbuf.at[j], qr.at[j])
    for d in range(S):
        arrived(kbuf.at[d], kr.at[d])
    scores = lax.dot_general(
        qbuf[...].reshape(mine, DH), kbuf[...].reshape(count, DH),
        (((1,), (1,)), ((), ())), preferred_element_type=jnp.float32,
    ) * (DH ** -0.5)
    scores = jnp.where(allowed, scores, NEG)
    peak = jnp.max(scores, axis=1, keepdims=True)
    expo = jnp.exp(scores - peak)
    total = jnp.sum(expo, axis=1, keepdims=True)
    for d in range(S):
        arrived(vbuf.at[d], vr.at[d])
    summed = jnp.dot(
        expo.astype(jnp.bfloat16), vbuf[...].reshape(count, DH),
        preferred_element_type=jnp.float32,
    )
    aown[...] = (summed / total).astype(jnp.bfloat16).reshape(H, rows, DH)

    for e in range(G):
        for jj in range(H):
            i = jj * G + e
            tgt = lax.rem(me + i, S)
            dst = abuf.at[g, :, :, lanes(head, DH)]
            if i == 0:
                pltpu.make_async_copy(aown, dst, ar.at[me]).start()
            else:
                send(aown, dst, as_.at[i], ar.at[me], tgt, z)
    loads[0].wait()

    for e in range(G):
        gg = lax.rem(g + e, G)
        for jj in range(H):
            src = lax.rem(head + jj, H) * G + gg
            arrived(aown, ar.at[src])
        product = jnp.dot(
            abuf[gg].reshape(mine, H * DH), ow[...], preferred_element_type=jnp.float32
        )
        cbuf[gg] = product.astype(jnp.bfloat16).reshape(H, rows, cols)
        for jj in range(H):
            j = lax.rem(head + jj, H)
            tgt = j * G + gg
            if e == 0 and jj == 0:
                pltpu.make_async_copy(cbuf.at[gg, j], rel.at[me], relr.at[me]).start()
            else:
                send(cbuf.at[gg, j], rel.at[me], cs.at[e * H + jj], relr.at[me], tgt, z)

    passed = []
    for e in range(G):
        for jj in range(H):
            src = lax.rem(head - jj + H, H) * G + lax.rem(g - e + G, G)
            chunk, place = src // CP, lax.rem(src, CP)
            arrived(rel.at[src], relr.at[src])
            dst, dsem = rbuf.at[z, place], cr.at[z, place]
            onward = pltpu.make_async_remote_copy(
                src_ref=rel.at[src], dst_ref=dst, send_sem=fs.at[e * H + jj], recv_sem=dsem,
                device_id={"seq": me, "tp": chunk}, device_id_type=MESH,
            )
            away = chunk != z
            pl.when(away)(onward.start)

            @pl.when(jnp.logical_not(away))
            def _():
                pltpu.make_async_copy(rel.at[src], dst, dsem).start()

            passed.append((away, onward))

    loads[1].wait()
    for t in range(T):
        for p in range(CP):
            arrived(rbuf.at[t, p], cr.at[t, p])
    for p in range(CP):
        mixed = rbuf[0, p].astype(jnp.float32)
        for t in range(1, T):
            mixed = mixed + rbuf[t, p].astype(jnp.float32)
        at = pl.ds(p * cols, cols)
        npbuf[:, at] = (ps[:, at].astype(jnp.float32) + mixed).astype(jnp.bfloat16)
    np_out = pltpu.make_async_copy(npbuf, np_hbm, loc.at[4])
    np_out.start()

    loads[2].wait()
    wide = dw.shape[1]
    padded = dbuf.shape[2]
    down = jnp.dot(npbuf[...], dw[...], preferred_element_type=jnp.float32)

    def share(x, t):
        turned = x if t == 0 else pltpu.roll(x, wide - t * local, 1)
        return turned[:, :padded].astype(jnp.bfloat16)

    for t in range(T):
        dsend[t] = share(down, t)
    for i in range(1, T):
        t = lax.rem(z + i, T)
        send(dsend.at[t], dbuf.at[z], ds_.at[i], dr.at[z], me, t)
    dbuf[z] = dsend[z]

    held = jnp.sum(valid8[:1, :], axis=1, keepdims=True)
    lane16 = lax.broadcasted_iota(jnp.int32, (16, rows), 1).astype(jnp.float32)
    pick = jnp.where(lane16 == held - 1.0, 1.0, 0.0).astype(jnp.bfloat16)
    last = jnp.dot(pick, down.astype(jnp.bfloat16), preferred_element_type=jnp.float32)
    for t in range(T):
        lsend[t] = share(last, t)
    after = lax.rem(me + 1, S)
    for i in range(T):
        t = lax.rem(z + i, T)
        send(lsend.at[t], lbuf.at[z], ls.at[i], lr.at[z], after, t)

    position = lax.broadcasted_iota(jnp.int32, (B_DEV, rows), 0)
    begun = jnp.where(st_ref[...] <= position, 1.0, 0.0)
    reached = jnp.sum(begun, axis=1, keepdims=True)
    lane_b = lax.broadcasted_iota(jnp.int32, (B_DEV, rows), 1).astype(jnp.float32)
    member = jnp.where(lane_b == reached - 1.0, 1.0, 0.0).astype(jnp.bfloat16)
    before = reached < 0.5
    loads[3].wait()

    for i in range(1, T):
        t = lax.rem(z + i, T)
        arrived(dbuf.at[t], dr.at[t])
    for t in range(T):
        arrived(lbuf.at[t], lr.at[t])
    state = dbuf[0].astype(jnp.float32)
    earlier = lbuf[0].astype(jnp.float32)
    for t in range(1, T):
        state = state + dbuf[t].astype(jnp.float32)
        earlier = earlier + lbuf[t].astype(jnp.float32)
    state = state.astype(jnp.bfloat16)
    earlier = earlier.astype(jnp.bfloat16).astype(jnp.float32)[:1, :]
    added = jnp.dot(member, state, preferred_element_type=jnp.float32)
    pd[...] = jnp.where(before, earlier, added)
    nb[...] = (bs[...].astype(jnp.float32) + pd[:, :local]).astype(jnp.bfloat16)
    nb_out = pltpu.make_async_copy(nb, nb_hbm, loc.at[5])
    nb_out.start()

    for copy in sends:
        copy.wait_send()

    for away, onward in passed:
        pl.when(away)(onward.wait_send)

    np_out.wait()
    nb_out.wait()


def fused_form(
    S, T, queries, keys, values, patch_stream, out_weight, down_weight, byte_states, patch_starts
):
    rows, width = queries.shape
    H = width // DH
    G = S // H
    cols = out_weight.shape[1]
    bytes_here, local = byte_states.shape
    padded = -(-local // 128) * 128
    bf = jnp.bfloat16
    sem = pltpu.SemaphoreType.DMA
    scratch = [
        pltpu.VMEM((H, rows, DH), bf),
        pltpu.VMEM((S, rows, DH), bf),
        pltpu.VMEM((S, rows, DH), bf),
        pltpu.VMEM((S, 8, rows), jnp.float32),
        pltpu.VMEM((H, rows, DH), bf),
        pltpu.VMEM((G, H, rows, width), bf),
        pltpu.VMEM((G, H, rows, cols), bf),
        pltpu.VMEM((S, rows, cols), bf),
        pltpu.VMEM((T, S // T, rows, cols), bf),
        pltpu.VMEM(patch_stream.shape, bf),
        pltpu.VMEM((T, rows, padded), bf),
        pltpu.VMEM((T, rows, padded), bf),
        pltpu.VMEM((T, 16, padded), bf),
        pltpu.VMEM((T, 16, padded), bf),
        pltpu.VMEM(out_weight.shape, bf),
        pltpu.VMEM(down_weight.shape, bf),
        pltpu.VMEM(patch_stream.shape, bf),
        pltpu.VMEM(byte_states.shape, bf),
        pltpu.VMEM((bytes_here, padded), jnp.float32),
        pltpu.VMEM(byte_states.shape, bf),
        sem((S,)), sem((H,)), sem((S,)), sem((S,)), sem((S,)), sem((S,)),
        sem((S,)), sem((S,)), sem((S,)), sem((S,)), sem((S,)), sem((S,)), sem((S,)),
        sem((T, S // T)),
        sem((T,)), sem((T,)), sem((T,)), sem((T,)), sem((6,)),
    ]
    hbm = pl.BlockSpec(memory_space=pl.ANY)
    return tuple(pl.pallas_call(
        functools.partial(fused_kernel, (S, T, H, rows, local)),
        out_shape=(
            jax.ShapeDtypeStruct(patch_stream.shape, bf),
            jax.ShapeDtypeStruct(byte_states.shape, bf),
        ),
        in_specs=[hbm] * 7 + [pl.BlockSpec(memory_space=pltpu.VMEM)],
        out_specs=(hbm, hbm),
        scratch_shapes=scratch,
        compiler_params=pltpu.CompilerParams(collective_id=0, has_side_effects=True),
    )(queries, keys, values, patch_stream, out_weight, down_weight, byte_states, patch_starts))


def on_device(S, T, *args):
    queries, out_weight = args[0], args[4]
    heads = queries.shape[1] // DH
    aligned = out_weight.shape[1] % 128 == 0 and queries.shape[0] % 16 == 0
    if aligned and S % heads == 0 and S % T == 0 and S >= T:
        return fused_form(S, T, *args)
    return plain_form(*args)


def solution(mesh):
    in_specs = (
        P("seq", "tp"),
        P("seq", "tp"),
        P("seq", "tp"),
        P("seq", "tp"),
        P("tp", "seq"),
        P("tp", None),
        P("seq", "tp"),
        P("seq", None),
    )
    out_specs = (P("seq", "tp"), P("seq", "tp"))
    return jax.shard_map(
        functools.partial(on_device, mesh.shape["seq"], mesh.shape["tp"]),
        mesh=mesh, in_specs=in_specs, out_specs=out_specs, check_vma=False
    )
```

```python
import functools

import jax
import jax.numpy as jnp
from jax import lax
from jax.experimental import pallas as pl
from jax.experimental.pallas import tpu as pltpu
from jax.sharding import PartitionSpec as P

DH = 128
B_DEV = 192


NEG = -1e30


def from_behind(value, axis, by):
    devices = lax.axis_size(axis)
    pairs = [(i, i + by) for i in range(devices) if 0 <= i + by < devices]
    return lax.ppermute(value, axis, pairs)


def plain_form(
    queries, keys, values, patch_stream, out_weight, down_weight, byte_states, patch_starts
):
    rows = queries.shape[0]
    width = queries.shape[1]
    heads = width // DH
    scale = DH ** (-0.5)
    starts_row = patch_starts.reshape(-1)
    valid = starts_row < B_DEV
    key_mask = valid.astype(jnp.bfloat16)
    first_slot = lax.axis_index("seq") * rows
    query_ids = first_slot + jnp.arange(rows, dtype=jnp.int32)
    query_heads = queries.reshape(rows, heads, DH)
    peak = jnp.full((heads, rows), NEG, jnp.float32)
    key_piece = lax.all_gather(keys, "seq", axis=0, tiled=True)
    value_piece = lax.all_gather(values, "seq", axis=0, tiled=True)
    mask_piece = lax.all_gather(key_mask, "seq", axis=0, tiled=True)
    count = key_piece.shape[0]
    key_heads = key_piece.reshape(count, heads, DH)
    value_heads = value_piece.reshape(count, heads, DH)
    scores = (
        jnp.einsum("qhd,khd->hqk", query_heads, key_heads, preferred_element_type=jnp.float32)
        * scale
    )
    key_ids = jnp.arange(count, dtype=jnp.int32)
    allowed = (mask_piece > 0)[None, :] & (key_ids[None, :] <= query_ids[:, None])
    scores = jnp.where(allowed[None], scores, NEG)
    new_peak = jnp.maximum(peak, jnp.max(scores, axis=-1))
    expo = jnp.exp(scores - new_peak[:, :, None])
    total = jnp.sum(expo, axis=-1)
    weights = expo.astype(jnp.bfloat16)
    summed = jnp.einsum("hqk,khd->hqd", weights, value_heads, preferred_element_type=jnp.float32)
    peak, total, summed = (new_peak, total, summed)
    attn = summed / total[:, :, None]
    attn = jnp.transpose(attn, (1, 0, 2)).reshape(rows, width).astype(jnp.bfloat16)
    partial_value = jnp.dot(
        attn,
        lax.all_gather(out_weight, "seq", axis=1, tiled=True),
        preferred_element_type=jnp.float32,
    )
    mixed = lax.psum_scatter(
        partial_value.astype(jnp.bfloat16), "tp", scatter_dimension=1, tiled=True
    ).astype(jnp.float32)
    new_patches = (patch_stream.astype(jnp.float32) + mixed).astype(jnp.bfloat16)
    down_terms = jnp.dot(new_patches, down_weight, preferred_element_type=jnp.float32)
    patch_down = lax.psum_scatter(
        down_terms.astype(jnp.bfloat16), "tp", scatter_dimension=1, tiled=True
    )
    following = jnp.concatenate([valid[1:], jnp.zeros((1,), jnp.bool_)])
    last_pick = (valid & jnp.logical_not(following)).astype(jnp.bfloat16)[None, :]
    last_state = jnp.dot(last_pick, patch_down, preferred_element_type=jnp.float32).astype(
        jnp.bfloat16
    )
    earlier_state = from_behind(last_state, "seq", 1)
    position = jnp.arange(B_DEV, dtype=jnp.int32)
    ends = jnp.concatenate([starts_row[1:], jnp.full((1,), B_DEV, jnp.int32)])
    member = (starts_row[None, :] <= position[:, None]) & (position[:, None] < ends[None, :])
    member = member.astype(jnp.bfloat16)
    before = (position < starts_row[0]).astype(jnp.float32)[:, None]
    added = jnp.dot(member, patch_down, preferred_element_type=jnp.float32)
    added = added + before * earlier_state.astype(jnp.float32)
    new_bytes = (byte_states.astype(jnp.float32) + added).astype(jnp.bfloat16)
    return (new_patches, new_bytes)


MESH = pl.DeviceIdType.MESH


def fused_kernel(
    sizes,
    q_hbm, k_hbm, v_hbm, ps_hbm, ow_hbm, dw_hbm, bs_hbm, st_ref,
    np_hbm, nb_hbm,
    qbuf, kbuf, vbuf, sbuf, aown, abuf, cbuf, rel, rbuf, npbuf, dsend, dbuf, lsend, lbuf,
    ow, dw, ps, bs, pd, nb,
    qs, qr, ks, kr, vs, vr, ss, sr, as_, ar, cs, relr, fs, cr, ds_, dr, ls, lr, loc, hello,
):
    S, T, H, rows, local = sizes
    G = S // H
    CP = S // T
    cols = ow.shape[1]
    me = lax.axis_index("seq")
    z = lax.axis_index("tp")
    head = me // G
    g = lax.rem(me, G)

    loads = [
        pltpu.make_async_copy(src, dst, loc.at[n])
        for n, (src, dst) in enumerate(
            ((ow_hbm, ow), (ps_hbm, ps), (dw_hbm, dw), (bs_hbm, bs))
        )
    ]
    for load in loads:
        load.start()

    starts = jnp.broadcast_to(st_ref[...], (8, rows))
    valid8 = jnp.where(starts < B_DEV, 1.0, 0.0)
    sbuf[me] = valid8

    barrier = pltpu.get_barrier_semaphore()
    for i in range(1, S):
        pl.semaphore_signal(
            barrier, inc=1, device_id={"seq": lax.rem(me + i, S), "tp": z}, device_id_type=MESH
        )

    def greet(sem):
        @pl.when(z > 0)
        def _():
            pl.semaphore_signal(
                sem, inc=1, device_id={"seq": me, "tp": z - 1}, device_id_type=MESH
            )

        @pl.when(z < T - 1)
        def _():
            pl.semaphore_signal(
                sem, inc=1, device_id={"seq": me, "tp": z + 1}, device_id_type=MESH
            )

    beside = jnp.where(z > 0, 1, 0) + jnp.where(z < T - 1, 1, 0)
    greet(barrier)
    pl.semaphore_wait(barrier, S - 1 + beside)
    if T > 2:
        greet(hello.at[0])

    def lanes(block, width):
        return pl.ds(pl.multiple_of(block * width, 128), width)

    sends = []

    def send(src, dst, ssem, rsem, seq, tp):
        copy = pltpu.make_async_remote_copy(
            src_ref=src, dst_ref=dst, send_sem=ssem, recv_sem=rsem,
            device_id={"seq": seq, "tp": tp}, device_id_type=MESH,
        )
        copy.start()
        sends.append(copy)

    def arrived(dst, sem):
        pltpu.make_async_copy(dst, dst, sem).wait()

    for i in range(S):
        tgt = lax.rem(me + i, S)
        part = lanes(tgt // G, DH)
        if i == 0:
            pltpu.make_async_copy(k_hbm.at[:, part], kbuf.at[me], kr.at[me]).start()
            pltpu.make_async_copy(v_hbm.at[:, part], vbuf.at[me], vr.at[me]).start()
            pltpu.make_async_copy(q_hbm.at[:, part], qbuf.at[head], qr.at[head]).start()
        else:
            send(k_hbm.at[:, part], kbuf.at[me], ks.at[i], kr.at[me], tgt, z)
            if i % G == 0:
                send(q_hbm.at[:, part], qbuf.at[head], qs.at[i], qr.at[head], tgt, z)
            send(sbuf.at[me], sbuf.at[me], ss.at[i], sr.at[me], tgt, z)
            send(v_hbm.at[:, part], vbuf.at[me], vs.at[i], vr.at[me], tgt, z)

    count = S * rows
    key_row = lax.broadcasted_iota(jnp.int32, (rows, count), 1)
    slot = lax.broadcasted_iota(jnp.int32, (rows, count), 0)
    spread = key_row == slot
    for d in range(1, S):
        spread = spread | (key_row == slot + d * rows)
    spread = jnp.where(spread, 1.0, 0.0).astype(jnp.bfloat16)

    for i in range(1, S):
        src = lax.rem(me + i, S)
        arrived(sbuf.at[src], sr.at[src])
    which = lax.broadcasted_iota(jnp.int32, (S, rows), 0)
    valid = jnp.zeros((S, rows), jnp.float32)
    for d in range(S):
        valid = jnp.where(which == d, sbuf[d][:1, :], valid)
    laid = jnp.dot(valid.astype(jnp.bfloat16), spread, preferred_element_type=jnp.float32)
    owner = lax.broadcasted_iota(jnp.int32, (S, count), 0) * rows
    lane = lax.broadcasted_iota(jnp.int32, (S, count), 1)
    laid = jnp.where((lane >= owner) & (lane < owner + rows), laid, 0.0)
    key_valid = jnp.sum(laid, axis=0, keepdims=True)

    mine = H * rows
    row = lax.broadcasted_iota(jnp.int32, (mine, count), 0)
    block = jnp.zeros((mine, count), jnp.int32)
    for j in range(1, H):
        block = block + jnp.where(row >= j * rows, (G - 1) * rows, 0)
    query = row + block + g * rows
    key = lax.broadcasted_iota(jnp.int32, (mine, count), 1)
    allowed = (key <= query) & (key_valid > 0.0)

    for j in range(H):
        arrived(qbuf.at[j], qr.at[j])
    for d in range(S):
        arrived(kbuf.at[d], kr.at[d])
    scores = lax.dot_general(
        qbuf[...].reshape(mine, DH), kbuf[...].reshape(count, DH),
        (((1,), (1,)), ((), ())), preferred_element_type=jnp.float32,
    ) * (DH ** -0.5)
    scores = jnp.where(allowed, scores, NEG)
    peak = jnp.max(scores, axis=1, keepdims=True)
    expo = jnp.exp(scores - peak)
    total = jnp.sum(expo, axis=1, keepdims=True)
    for d in range(S):
        arrived(vbuf.at[d], vr.at[d])
    summed = jnp.dot(
        expo.astype(jnp.bfloat16), vbuf[...].reshape(count, DH),
        preferred_element_type=jnp.float32,
    )
    aown[...] = (summed / total).astype(jnp.bfloat16).reshape(H, rows, DH)

    own = abuf.at[g, :, :, lanes(head, DH)]
    pltpu.make_async_copy(aown, own, ar.at[me]).start()
    for jj in range(1, H):
        tgt = lax.rem(head + jj, H) * G + g
        send(aown, own, as_.at[jj * G], ar.at[me], tgt, z)
    for e in range(1, G):
        send(aown, own, as_.at[e], ar.at[me], head * G + lax.rem(g + e, G), z)
    for n in range(1, T - 2):
        pl.semaphore_wait(hello.at[n - 1], beside)
        greet(hello.at[n])
    loads[0].wait()

    for e in range(G):
        gg = lax.rem(g + e, G)
        for jj in range(H):
            h = lax.rem(head - jj + H, H)
            src = h * G + gg
            arrived(aown, ar.at[src])
            if e == 0 and jj > 0:
                piece = abuf.at[g, :, :, lanes(h, DH)]
                for f in range(1, G):
                    partner = head * G + lax.rem(g + f, G)
                    send(piece, piece, as_.at[jj * G + f], ar.at[src], partner, z)
        product = jnp.dot(
            abuf[gg].reshape(mine, H * DH), ow[...], preferred_element_type=jnp.float32
        )
        cbuf[gg] = product.astype(jnp.bfloat16).reshape(H, rows, cols)
        for jj in range(H):
            j = lax.rem(head + jj, H)
            tgt = j * G + gg
            if e == 0 and jj == 0:
                pltpu.make_async_copy(cbuf.at[gg, j], rel.at[me], relr.at[me]).start()
            else:
                send(cbuf.at[gg, j], rel.at[me], cs.at[e * H + jj], relr.at[me], tgt, z)

    if T > 2:
        pl.semaphore_wait(hello.at[T - 3], beside)
    passed = []
    for e in range(G):
        for jj in range(H):
            src = lax.rem(head - jj + H, H) * G + lax.rem(g - e + G, G)
            chunk, place = src // CP, lax.rem(src, CP)
            arrived(rel.at[src], relr.at[src])
            dst, dsem = rbuf.at[z, place], cr.at[z, place]
            onward = pltpu.make_async_remote_copy(
                src_ref=rel.at[src], dst_ref=dst, send_sem=fs.at[e * H + jj], recv_sem=dsem,
                device_id={"seq": me, "tp": chunk}, device_id_type=MESH,
            )
            away = chunk != z
            pl.when(away)(onward.start)

            @pl.when(jnp.logical_not(away))
            def _():
                pltpu.make_async_copy(rel.at[src], dst, dsem).start()

            passed.append((away, onward))

    loads[1].wait()
    for t in range(T):
        for p in range(CP):
            arrived(rbuf.at[t, p], cr.at[t, p])
    for p in range(CP):
        mixed = rbuf[0, p].astype(jnp.float32)
        for t in range(1, T):
            mixed = mixed + rbuf[t, p].astype(jnp.float32)
        at = pl.ds(p * cols, cols)
        npbuf[:, at] = (ps[:, at].astype(jnp.float32) + mixed).astype(jnp.bfloat16)
    np_out = pltpu.make_async_copy(npbuf, np_hbm, loc.at[4])
    np_out.start()

    loads[2].wait()
    wide = dw.shape[1]
    padded = dbuf.shape[2]
    down = jnp.dot(npbuf[...], dw[...], preferred_element_type=jnp.float32)

    def turned(x, t):
        return (x if t == 0 else pltpu.roll(x, wide - t * local, 1))[:, :padded]

    for t in range(T):
        dsend[t] = turned(down, t).astype(jnp.bfloat16)
    for i in range(1, T):
        t = lax.rem(z + i, T)
        send(dsend.at[t], dbuf.at[z], ds_.at[i], dr.at[z], me, t)
    dbuf[z] = dsend[z]

    held = jnp.sum(valid8[:1, :], axis=1, keepdims=True)
    lane16 = lax.broadcasted_iota(jnp.int32, (16, rows), 1).astype(jnp.float32)
    pick = jnp.where(lane16 == held - 1.0, 1.0, 0.0).astype(jnp.bfloat16)
    last = jnp.dot(pick, down.astype(jnp.bfloat16), preferred_element_type=jnp.float32)
    for t in range(T):
        lsend[t] = turned(last, t)[:1, :]
    after = lax.rem(me + 1, S)
    for i in range(T):
        t = lax.rem(z + i, T)
        send(lsend.at[t], lbuf.at[z], ls.at[i], lr.at[z], after, t)

    position = lax.broadcasted_iota(jnp.int32, (B_DEV, rows), 0)
    begun = jnp.where(st_ref[...] <= position, 1.0, 0.0)
    reached = jnp.sum(begun, axis=1, keepdims=True)
    lane_b = lax.broadcasted_iota(jnp.int32, (B_DEV, rows), 1).astype(jnp.float32)
    member = jnp.where(lane_b == reached - 1.0, 1.0, 0.0).astype(jnp.bfloat16)
    before = reached < 0.5
    loads[3].wait()

    for i in range(1, T):
        t = lax.rem(z + i, T)
        arrived(dbuf.at[t], dr.at[t])
    for t in range(T):
        arrived(lbuf.at[t], lr.at[t])
    state = dbuf[0].astype(jnp.float32)
    earlier = lbuf[0]
    for t in range(1, T):
        state = state + dbuf[t].astype(jnp.float32)
        earlier = earlier + lbuf[t]
    state = state.astype(jnp.bfloat16)
    earlier = earlier.astype(jnp.bfloat16).astype(jnp.float32)
    added = jnp.dot(member, state, preferred_element_type=jnp.float32)
    pd[...] = jnp.where(before, earlier, added)
    nb[...] = (bs[...].astype(jnp.float32) + pd[:, :local]).astype(jnp.bfloat16)
    nb_out = pltpu.make_async_copy(nb, nb_hbm, loc.at[5])
    nb_out.start()

    for copy in sends:
        copy.wait_send()

    for away, onward in passed:
        pl.when(away)(onward.wait_send)

    np_out.wait()
    nb_out.wait()


def fused_form(
    S, T, queries, keys, values, patch_stream, out_weight, down_weight, byte_states, patch_starts
):
    rows, width = queries.shape
    H = width // DH
    G = S // H
    cols = out_weight.shape[1]
    bytes_here, local = byte_states.shape
    padded = -(-local // 128) * 128
    bf = jnp.bfloat16
    sem = pltpu.SemaphoreType.DMA
    scratch = [
        pltpu.VMEM((H, rows, DH), bf),
        pltpu.VMEM((S, rows, DH), bf),
        pltpu.VMEM((S, rows, DH), bf),
        pltpu.VMEM((S, 8, rows), jnp.float32),
        pltpu.VMEM((H, rows, DH), bf),
        pltpu.VMEM((G, H, rows, width), bf),
        pltpu.VMEM((G, H, rows, cols), bf),
        pltpu.VMEM((S, rows, cols), bf),
        pltpu.VMEM((T, S // T, rows, cols), bf),
        pltpu.VMEM(patch_stream.shape, bf),
        pltpu.VMEM((T, rows, padded), bf),
        pltpu.VMEM((T, rows, padded), bf),
        pltpu.VMEM((T, 1, padded), jnp.float32),
        pltpu.VMEM((T, 1, padded), jnp.float32),
        pltpu.VMEM(out_weight.shape, bf),
        pltpu.VMEM(down_weight.shape, bf),
        pltpu.VMEM(patch_stream.shape, bf),
        pltpu.VMEM(byte_states.shape, bf),
        pltpu.VMEM((bytes_here, padded), jnp.float32),
        pltpu.VMEM(byte_states.shape, bf),
        sem((S,)), sem((H,)), sem((S,)), sem((S,)), sem((S,)), sem((S,)),
        sem((S,)), sem((S,)), sem((S,)), sem((S,)), sem((S,)), sem((S,)), sem((S,)),
        sem((T, S // T)),
        sem((T,)), sem((T,)), sem((T,)), sem((T,)), sem((6,)),
        pltpu.SemaphoreType.REGULAR((max(T - 2, 1),)),
    ]
    hbm = pl.BlockSpec(memory_space=pl.ANY)
    return tuple(pl.pallas_call(
        functools.partial(fused_kernel, (S, T, H, rows, local)),
        out_shape=(
            jax.ShapeDtypeStruct(patch_stream.shape, bf),
            jax.ShapeDtypeStruct(byte_states.shape, bf),
        ),
        in_specs=[hbm] * 7 + [pl.BlockSpec(memory_space=pltpu.VMEM)],
        out_specs=(hbm, hbm),
        scratch_shapes=scratch,
        compiler_params=pltpu.CompilerParams(collective_id=0, has_side_effects=True),
    )(queries, keys, values, patch_stream, out_weight, down_weight, byte_states, patch_starts))


def on_device(S, T, *args):
    queries, out_weight = args[0], args[4]
    heads = queries.shape[1] // DH
    aligned = out_weight.shape[1] % 128 == 0 and queries.shape[0] % 16 == 0
    if aligned and S % heads == 0 and S % T == 0 and S >= T:
        return fused_form(S, T, *args)
    return plain_form(*args)


def solution(mesh):
    in_specs = (
        P("seq", "tp"),
        P("seq", "tp"),
        P("seq", "tp"),
        P("seq", "tp"),
        P("tp", "seq"),
        P("tp", None),
        P("seq", "tp"),
        P("seq", None),
    )
    out_specs = (P("seq", "tp"), P("seq", "tp"))
    return jax.shard_map(
        functools.partial(on_device, mesh.shape["seq"], mesh.shape["tp"]),
        mesh=mesh, in_specs=in_specs, out_specs=out_specs, check_vma=False
    )
```

```python
import functools

import jax
import jax.numpy as jnp
from jax import lax
from jax.experimental import pallas as pl
from jax.experimental.pallas import tpu as pltpu
from jax.sharding import PartitionSpec as P

DH = 128
B_DEV = 192


NEG = -1e30


def from_behind(value, axis, by):
    devices = lax.axis_size(axis)
    pairs = [(i, i + by) for i in range(devices) if 0 <= i + by < devices]
    return lax.ppermute(value, axis, pairs)


def plain_form(
    queries, keys, values, patch_stream, out_weight, down_weight, byte_states, patch_starts
):
    rows = queries.shape[0]
    width = queries.shape[1]
    heads = width // DH
    scale = DH ** (-0.5)
    starts_row = patch_starts.reshape(-1)
    valid = starts_row < B_DEV
    key_mask = valid.astype(jnp.bfloat16)
    first_slot = lax.axis_index("seq") * rows
    query_ids = first_slot + jnp.arange(rows, dtype=jnp.int32)
    query_heads = queries.reshape(rows, heads, DH)
    peak = jnp.full((heads, rows), NEG, jnp.float32)
    key_piece = lax.all_gather(keys, "seq", axis=0, tiled=True)
    value_piece = lax.all_gather(values, "seq", axis=0, tiled=True)
    mask_piece = lax.all_gather(key_mask, "seq", axis=0, tiled=True)
    count = key_piece.shape[0]
    key_heads = key_piece.reshape(count, heads, DH)
    value_heads = value_piece.reshape(count, heads, DH)
    scores = (
        jnp.einsum("qhd,khd->hqk", query_heads, key_heads, preferred_element_type=jnp.float32)
        * scale
    )
    key_ids = jnp.arange(count, dtype=jnp.int32)
    allowed = (mask_piece > 0)[None, :] & (key_ids[None, :] <= query_ids[:, None])
    scores = jnp.where(allowed[None], scores, NEG)
    new_peak = jnp.maximum(peak, jnp.max(scores, axis=-1))
    expo = jnp.exp(scores - new_peak[:, :, None])
    total = jnp.sum(expo, axis=-1)
    weights = expo.astype(jnp.bfloat16)
    summed = jnp.einsum("hqk,khd->hqd", weights, value_heads, preferred_element_type=jnp.float32)
    peak, total, summed = (new_peak, total, summed)
    attn = summed / total[:, :, None]
    attn = jnp.transpose(attn, (1, 0, 2)).reshape(rows, width).astype(jnp.bfloat16)
    partial_value = jnp.dot(
        attn,
        lax.all_gather(out_weight, "seq", axis=1, tiled=True),
        preferred_element_type=jnp.float32,
    )
    mixed = lax.psum_scatter(
        partial_value.astype(jnp.bfloat16), "tp", scatter_dimension=1, tiled=True
    ).astype(jnp.float32)
    new_patches = (patch_stream.astype(jnp.float32) + mixed).astype(jnp.bfloat16)
    down_terms = jnp.dot(new_patches, down_weight, preferred_element_type=jnp.float32)
    patch_down = lax.psum_scatter(
        down_terms.astype(jnp.bfloat16), "tp", scatter_dimension=1, tiled=True
    )
    following = jnp.concatenate([valid[1:], jnp.zeros((1,), jnp.bool_)])
    last_pick = (valid & jnp.logical_not(following)).astype(jnp.bfloat16)[None, :]
    last_state = jnp.dot(last_pick, patch_down, preferred_element_type=jnp.float32).astype(
        jnp.bfloat16
    )
    earlier_state = from_behind(last_state, "seq", 1)
    position = jnp.arange(B_DEV, dtype=jnp.int32)
    ends = jnp.concatenate([starts_row[1:], jnp.full((1,), B_DEV, jnp.int32)])
    member = (starts_row[None, :] <= position[:, None]) & (position[:, None] < ends[None, :])
    member = member.astype(jnp.bfloat16)
    before = (position < starts_row[0]).astype(jnp.float32)[:, None]
    added = jnp.dot(member, patch_down, preferred_element_type=jnp.float32)
    added = added + before * earlier_state.astype(jnp.float32)
    new_bytes = (byte_states.astype(jnp.float32) + added).astype(jnp.bfloat16)
    return (new_patches, new_bytes)


MESH = pl.DeviceIdType.MESH


def fused_kernel(
    sizes,
    q_hbm, k_hbm, v_hbm, ps_hbm, ow_hbm, dw_hbm, bs_hbm, st_hbm,
    np_out, nb_out,
    qbuf, kbuf, vbuf, sbuf, aown, abuf, cbuf, rel, rbuf, dsend, dbuf, lsend, lbuf,
    ow, dw, ps, bs, pd, st_ref,
    qs, qr, ks, kr, vs, vr, ss, sr, as_, ar, cs, relr, fs, cr, ds_, dr, ls, lr, loc, hello,
):
    S, T, H, rows, local = sizes
    G = S // H
    CP = S // T
    cols = ow.shape[1]
    me = lax.axis_index("seq")
    z = lax.axis_index("tp")
    head = me // G
    g = lax.rem(me, G)

    loads = [
        pltpu.make_async_copy(src, dst, loc.at[n])
        for n, (src, dst) in enumerate(
            ((ow_hbm, ow), (ps_hbm, ps), (dw_hbm, dw), (bs_hbm, bs))
        )
    ]
    for load in loads:
        load.start()

    first = pltpu.make_async_copy(st_hbm, st_ref, loc.at[4])
    first.start()
    barrier = pltpu.get_barrier_semaphore()
    for i in range(1, S):
        pl.semaphore_signal(
            barrier, inc=1, device_id={"seq": lax.rem(me + i, S), "tp": z}, device_id_type=MESH
        )

    def greet(sem):
        @pl.when(z > 0)
        def _():
            pl.semaphore_signal(
                sem, inc=1, device_id={"seq": me, "tp": z - 1}, device_id_type=MESH
            )

        @pl.when(z < T - 1)
        def _():
            pl.semaphore_signal(
                sem, inc=1, device_id={"seq": me, "tp": z + 1}, device_id_type=MESH
            )

    beside = jnp.where(z > 0, 1, 0) + jnp.where(z < T - 1, 1, 0)
    greet(barrier)
    first.wait()
    starts = jnp.broadcast_to(st_ref[...], (8, rows))
    valid8 = jnp.where(starts < B_DEV, 1.0, 0.0)
    sbuf[me] = valid8

    pl.semaphore_wait(barrier, S - 1 + beside)
    if T > 2:
        greet(hello.at[0])

    def lanes(block, width):
        return pl.ds(pl.multiple_of(block * width, 128), width)

    sends = []

    def send(src, dst, ssem, rsem, seq, tp):
        copy = pltpu.make_async_remote_copy(
            src_ref=src, dst_ref=dst, send_sem=ssem, recv_sem=rsem,
            device_id={"seq": seq, "tp": tp}, device_id_type=MESH,
        )
        copy.start()
        sends.append(copy)

    def arrived(dst, sem):
        pltpu.make_async_copy(dst, dst, sem).wait()

    for i in range(S):
        tgt = lax.rem(me + i, S)
        part = lanes(tgt // G, DH)
        if i == 0:
            pltpu.make_async_copy(k_hbm.at[:, part], kbuf.at[me], kr.at[me]).start()
            pltpu.make_async_copy(v_hbm.at[:, part], vbuf.at[me], vr.at[me]).start()
            pltpu.make_async_copy(q_hbm.at[:, part], qbuf.at[head], qr.at[head]).start()
        else:
            send(k_hbm.at[:, part], kbuf.at[me], ks.at[i], kr.at[me], tgt, z)
            if i % G == 0:
                send(q_hbm.at[:, part], qbuf.at[head], qs.at[i], qr.at[head], tgt, z)
            send(sbuf.at[me], sbuf.at[me], ss.at[i], sr.at[me], tgt, z)
            send(v_hbm.at[:, part], vbuf.at[me], vs.at[i], vr.at[me], tgt, z)

    count = S * rows
    key_row = lax.broadcasted_iota(jnp.int32, (rows, count), 1)
    slot = lax.broadcasted_iota(jnp.int32, (rows, count), 0)
    spread = key_row == slot
    for d in range(1, S):
        spread = spread | (key_row == slot + d * rows)
    spread = jnp.where(spread, 1.0, 0.0).astype(jnp.bfloat16)

    for i in range(1, S):
        src = lax.rem(me + i, S)
        arrived(sbuf.at[src], sr.at[src])
    which = lax.broadcasted_iota(jnp.int32, (S, rows), 0)
    valid = jnp.zeros((S, rows), jnp.float32)
    for d in range(S):
        valid = jnp.where(which == d, sbuf[d][:1, :], valid)
    laid = jnp.dot(valid.astype(jnp.bfloat16), spread, preferred_element_type=jnp.float32)
    owner = lax.broadcasted_iota(jnp.int32, (S, count), 0) * rows
    lane = lax.broadcasted_iota(jnp.int32, (S, count), 1)
    laid = jnp.where((lane >= owner) & (lane < owner + rows), laid, 0.0)
    key_valid = jnp.sum(laid, axis=0, keepdims=True)

    mine = H * rows
    row = lax.broadcasted_iota(jnp.int32, (mine, count), 0)
    block = jnp.zeros((mine, count), jnp.int32)
    for j in range(1, H):
        block = block + jnp.where(row >= j * rows, (G - 1) * rows, 0)
    query = row + block + g * rows
    key = lax.broadcasted_iota(jnp.int32, (mine, count), 1)
    allowed = (key <= query) & (key_valid > 0.0)

    for j in range(H):
        arrived(qbuf.at[j], qr.at[j])
    for d in range(S):
        arrived(kbuf.at[d], kr.at[d])
    scores = lax.dot_general(
        qbuf[...].reshape(mine, DH), kbuf[...].reshape(count, DH),
        (((1,), (1,)), ((), ())), preferred_element_type=jnp.float32,
    ) * (DH ** -0.5)
    scores = jnp.where(allowed, scores, NEG)
    peak = jnp.max(scores, axis=1, keepdims=True)
    expo = jnp.exp(scores - peak)
    total = jnp.sum(expo, axis=1, keepdims=True)
    for d in range(S):
        arrived(vbuf.at[d], vr.at[d])
    summed = jnp.dot(
        expo.astype(jnp.bfloat16), vbuf[...].reshape(count, DH),
        preferred_element_type=jnp.float32,
    )
    aown[...] = (summed / total).astype(jnp.bfloat16).reshape(H, rows, DH)

    own = abuf.at[g, :, :, lanes(head, DH)]
    pltpu.make_async_copy(aown, own, ar.at[me]).start()
    for jj in range(1, H):
        tgt = lax.rem(head + jj, H) * G + g
        send(aown, own, as_.at[jj * G], ar.at[me], tgt, z)
    for e in range(1, G):
        send(aown, own, as_.at[e], ar.at[me], head * G + lax.rem(g + e, G), z)
    for n in range(1, T - 2):
        pl.semaphore_wait(hello.at[n - 1], beside)
        greet(hello.at[n])
    loads[0].wait()

    for e in range(G):
        gg = lax.rem(g + e, G)
        for jj in range(H):
            h = lax.rem(head - jj + H, H)
            src = h * G + gg
            arrived(aown, ar.at[src])
            if e == 0 and jj > 0:
                piece = abuf.at[g, :, :, lanes(h, DH)]
                for f in range(1, G):
                    partner = head * G + lax.rem(g + f, G)
                    send(piece, piece, as_.at[jj * G + f], ar.at[src], partner, z)
        product = jnp.dot(
            abuf[gg].reshape(mine, H * DH), ow[...], preferred_element_type=jnp.float32
        )
        cbuf[gg] = product.astype(jnp.bfloat16).reshape(H, rows, cols)
        for jj in range(H):
            j = lax.rem(head + jj, H)
            tgt = j * G + gg
            if e == 0 and jj == 0:
                pltpu.make_async_copy(cbuf.at[gg, j], rel.at[me], relr.at[me]).start()
            else:
                send(cbuf.at[gg, j], rel.at[me], cs.at[e * H + jj], relr.at[me], tgt, z)

    if T > 2:
        pl.semaphore_wait(hello.at[T - 3], beside)
    passed = []
    for e in range(G):
        for jj in range(H):
            src = lax.rem(head - jj + H, H) * G + lax.rem(g - e + G, G)
            chunk, place = src // CP, lax.rem(src, CP)
            arrived(rel.at[src], relr.at[src])
            dst, dsem = rbuf.at[z, place], cr.at[z, place]
            onward = pltpu.make_async_remote_copy(
                src_ref=rel.at[src], dst_ref=dst, send_sem=fs.at[e * H + jj], recv_sem=dsem,
                device_id={"seq": me, "tp": chunk}, device_id_type=MESH,
            )
            away = chunk != z
            pl.when(away)(onward.start)

            @pl.when(jnp.logical_not(away))
            def _():
                pltpu.make_async_copy(rel.at[src], dst, dsem).start()

            passed.append((away, onward))

    loads[1].wait()
    for t in range(T):
        for p in range(CP):
            arrived(rbuf.at[t, p], cr.at[t, p])
    for p in range(CP):
        mixed = rbuf[0, p].astype(jnp.float32)
        for t in range(1, T):
            mixed = mixed + rbuf[t, p].astype(jnp.float32)
        at = pl.ds(p * cols, cols)
        np_out[:, at] = (ps[:, at].astype(jnp.float32) + mixed).astype(jnp.bfloat16)

    loads[2].wait()
    wide = dw.shape[1]
    padded = dbuf.shape[2]
    down = jnp.dot(np_out[...], dw[...], preferred_element_type=jnp.float32)

    def turned(x, t):
        return (x if t == 0 else pltpu.roll(x, wide - t * local, 1))[:, :padded]

    for t in range(T):
        dsend[t] = turned(down, t).astype(jnp.bfloat16)
    for i in range(1, T):
        t = lax.rem(z + i, T)
        send(dsend.at[t], dbuf.at[z], ds_.at[i], dr.at[z], me, t)
    dbuf[z] = dsend[z]

    held = jnp.sum(valid8[:1, :], axis=1, keepdims=True)
    lane16 = lax.broadcasted_iota(jnp.int32, (16, rows), 1).astype(jnp.float32)
    pick = jnp.where(lane16 == held - 1.0, 1.0, 0.0).astype(jnp.bfloat16)
    last = jnp.dot(pick, down.astype(jnp.bfloat16), preferred_element_type=jnp.float32)
    for t in range(T):
        lsend[t] = turned(last, t)[:1, :]
    after = lax.rem(me + 1, S)
    for i in range(T):
        t = lax.rem(z + i, T)
        send(lsend.at[t], lbuf.at[z], ls.at[i], lr.at[z], after, t)

    position = lax.broadcasted_iota(jnp.int32, (B_DEV, rows), 0)
    begun = jnp.where(st_ref[...] <= position, 1.0, 0.0)
    reached = jnp.sum(begun, axis=1, keepdims=True)
    lane_b = lax.broadcasted_iota(jnp.int32, (B_DEV, rows), 1).astype(jnp.float32)
    member = jnp.where(lane_b == reached - 1.0, 1.0, 0.0).astype(jnp.bfloat16)
    before = reached < 0.5
    loads[3].wait()

    for i in range(1, T):
        t = lax.rem(z + i, T)
        arrived(dbuf.at[t], dr.at[t])
    for t in range(T):
        arrived(lbuf.at[t], lr.at[t])
    state = dbuf[0].astype(jnp.float32)
    earlier = lbuf[0]
    for t in range(1, T):
        state = state + dbuf[t].astype(jnp.float32)
        earlier = earlier + lbuf[t]
    state = state.astype(jnp.bfloat16)
    earlier = earlier.astype(jnp.bfloat16).astype(jnp.float32)
    added = jnp.dot(member, state, preferred_element_type=jnp.float32)
    pd[...] = jnp.where(before, earlier, added)
    nb_out[...] = (bs[...].astype(jnp.float32) + pd[:, :local]).astype(jnp.bfloat16)

    for copy in sends:
        copy.wait_send()

    for away, onward in passed:
        pl.when(away)(onward.wait_send)


def put_out(np_ref, nb_ref, np_hbm, nb_hbm, sems):
    copies = [
        pltpu.make_async_copy(np_ref, np_hbm, sems.at[0]),
        pltpu.make_async_copy(nb_ref, nb_hbm, sems.at[1]),
    ]
    for copy in copies:
        copy.start()
    for copy in copies:
        copy.wait()


def fused_form(
    S, T, queries, keys, values, patch_stream, out_weight, down_weight, byte_states, patch_starts
):
    rows, width = queries.shape
    H = width // DH
    G = S // H
    cols = out_weight.shape[1]
    bytes_here, local = byte_states.shape
    padded = -(-local // 128) * 128
    bf = jnp.bfloat16
    sem = pltpu.SemaphoreType.DMA
    scratch = [
        pltpu.VMEM((H, rows, DH), bf),
        pltpu.VMEM((S, rows, DH), bf),
        pltpu.VMEM((S, rows, DH), bf),
        pltpu.VMEM((S, 8, rows), jnp.float32),
        pltpu.VMEM((H, rows, DH), bf),
        pltpu.VMEM((G, H, rows, width), bf),
        pltpu.VMEM((G, H, rows, cols), bf),
        pltpu.VMEM((S, rows, cols), bf),
        pltpu.VMEM((T, S // T, rows, cols), bf),
        pltpu.VMEM((T, rows, padded), bf),
        pltpu.VMEM((T, rows, padded), bf),
        pltpu.VMEM((T, 1, padded), jnp.float32),
        pltpu.VMEM((T, 1, padded), jnp.float32),
        pltpu.VMEM(out_weight.shape, bf),
        pltpu.VMEM(down_weight.shape, bf),
        pltpu.VMEM(patch_stream.shape, bf),
        pltpu.VMEM(byte_states.shape, bf),
        pltpu.VMEM((bytes_here, padded), jnp.float32),
        pltpu.VMEM(patch_starts.shape, jnp.int32),
        sem((S,)), sem((H,)), sem((S,)), sem((S,)), sem((S,)), sem((S,)),
        sem((S,)), sem((S,)), sem((S,)), sem((S,)), sem((S,)), sem((S,)), sem((S,)),
        sem((T, S // T)),
        sem((T,)), sem((T,)), sem((T,)), sem((T,)), sem((5,)),
        pltpu.SemaphoreType.REGULAR((max(T - 2, 1),)),
    ]
    hbm = pl.BlockSpec(memory_space=pltpu.HBM)
    vmem = pl.BlockSpec(memory_space=pltpu.VMEM)
    held = pl.pallas_call(
        functools.partial(fused_kernel, (S, T, H, rows, local)),
        out_shape=(
            jax.ShapeDtypeStruct(patch_stream.shape, bf),
            jax.ShapeDtypeStruct(byte_states.shape, bf),
        ),
        in_specs=[hbm] * 8,
        out_specs=(vmem, vmem),
        scratch_shapes=scratch,
        compiler_params=pltpu.CompilerParams(collective_id=0, has_side_effects=True, vmem_limit_bytes=24 << 20),
    )(*(
        pltpu.with_memory_space_constraint(x, pltpu.HBM)
        for x in (
            queries, keys, values, patch_stream,
            out_weight, down_weight, byte_states, patch_starts,
        )
    ))
    return tuple(pl.pallas_call(
        put_out,
        out_shape=(
            jax.ShapeDtypeStruct(patch_stream.shape, bf),
            jax.ShapeDtypeStruct(byte_states.shape, bf),
        ),
        in_specs=[vmem, vmem],
        out_specs=(hbm, hbm),
        scratch_shapes=[sem((2,))],
        compiler_params=pltpu.CompilerParams(vmem_limit_bytes=4 << 20),
    )(*held))


def on_device(S, T, *args):
    queries, out_weight = args[0], args[4]
    heads = queries.shape[1] // DH
    aligned = out_weight.shape[1] % 128 == 0 and queries.shape[0] % 16 == 0
    if aligned and S % heads == 0 and S % T == 0 and S >= T:
        return fused_form(S, T, *args)
    return plain_form(*args)


def solution(mesh):
    in_specs = (
        P("seq", "tp"),
        P("seq", "tp"),
        P("seq", "tp"),
        P("seq", "tp"),
        P("tp", "seq"),
        P("tp", None),
        P("seq", "tp"),
        P("seq", None),
    )
    out_specs = (P("seq", "tp"), P("seq", "tp"))
    return jax.shard_map(
        functools.partial(on_device, mesh.shape["seq"], mesh.shape["tp"]),
        mesh=mesh, in_specs=in_specs, out_specs=out_specs, check_vma=False
    )
```

```python
import functools

import jax
import jax.numpy as jnp
from jax import lax
from jax.experimental import pallas as pl
from jax.experimental.pallas import tpu as pltpu
from jax.sharding import PartitionSpec as P

DH = 128
B_DEV = 192


NEG = -1e30


def from_behind(value, axis, by):
    devices = lax.axis_size(axis)
    pairs = [(i, i + by) for i in range(devices) if 0 <= i + by < devices]
    return lax.ppermute(value, axis, pairs)


def plain_form(
    queries, keys, values, patch_stream, out_weight, down_weight, byte_states, patch_starts
):
    rows = queries.shape[0]
    width = queries.shape[1]
    heads = width // DH
    scale = DH ** (-0.5)
    starts_row = patch_starts.reshape(-1)
    valid = starts_row < B_DEV
    key_mask = valid.astype(jnp.bfloat16)
    first_slot = lax.axis_index("seq") * rows
    query_ids = first_slot + jnp.arange(rows, dtype=jnp.int32)
    query_heads = queries.reshape(rows, heads, DH)
    peak = jnp.full((heads, rows), NEG, jnp.float32)
    key_piece = lax.all_gather(keys, "seq", axis=0, tiled=True)
    value_piece = lax.all_gather(values, "seq", axis=0, tiled=True)
    mask_piece = lax.all_gather(key_mask, "seq", axis=0, tiled=True)
    count = key_piece.shape[0]
    key_heads = key_piece.reshape(count, heads, DH)
    value_heads = value_piece.reshape(count, heads, DH)
    scores = (
        jnp.einsum("qhd,khd->hqk", query_heads, key_heads, preferred_element_type=jnp.float32)
        * scale
    )
    key_ids = jnp.arange(count, dtype=jnp.int32)
    allowed = (mask_piece > 0)[None, :] & (key_ids[None, :] <= query_ids[:, None])
    scores = jnp.where(allowed[None], scores, NEG)
    new_peak = jnp.maximum(peak, jnp.max(scores, axis=-1))
    expo = jnp.exp(scores - new_peak[:, :, None])
    total = jnp.sum(expo, axis=-1)
    weights = expo.astype(jnp.bfloat16)
    summed = jnp.einsum("hqk,khd->hqd", weights, value_heads, preferred_element_type=jnp.float32)
    peak, total, summed = (new_peak, total, summed)
    attn = summed / total[:, :, None]
    attn = jnp.transpose(attn, (1, 0, 2)).reshape(rows, width).astype(jnp.bfloat16)
    partial_value = jnp.dot(
        attn,
        lax.all_gather(out_weight, "seq", axis=1, tiled=True),
        preferred_element_type=jnp.float32,
    )
    mixed = lax.psum_scatter(
        partial_value.astype(jnp.bfloat16), "tp", scatter_dimension=1, tiled=True
    ).astype(jnp.float32)
    new_patches = (patch_stream.astype(jnp.float32) + mixed).astype(jnp.bfloat16)
    down_terms = jnp.dot(new_patches, down_weight, preferred_element_type=jnp.float32)
    patch_down = lax.psum_scatter(
        down_terms.astype(jnp.bfloat16), "tp", scatter_dimension=1, tiled=True
    )
    following = jnp.concatenate([valid[1:], jnp.zeros((1,), jnp.bool_)])
    last_pick = (valid & jnp.logical_not(following)).astype(jnp.bfloat16)[None, :]
    last_state = jnp.dot(last_pick, patch_down, preferred_element_type=jnp.float32).astype(
        jnp.bfloat16
    )
    earlier_state = from_behind(last_state, "seq", 1)
    position = jnp.arange(B_DEV, dtype=jnp.int32)
    ends = jnp.concatenate([starts_row[1:], jnp.full((1,), B_DEV, jnp.int32)])
    member = (starts_row[None, :] <= position[:, None]) & (position[:, None] < ends[None, :])
    member = member.astype(jnp.bfloat16)
    before = (position < starts_row[0]).astype(jnp.float32)[:, None]
    added = jnp.dot(member, patch_down, preferred_element_type=jnp.float32)
    added = added + before * earlier_state.astype(jnp.float32)
    new_bytes = (byte_states.astype(jnp.float32) + added).astype(jnp.bfloat16)
    return (new_patches, new_bytes)


MESH = pl.DeviceIdType.MESH


def fused_kernel(
    sizes,
    q_hbm, k_hbm, v_hbm, ps_hbm, ow_hbm, dw_hbm, bs_hbm, st_hbm,
    np_out, nb_out,
    qbuf, kbuf, vbuf, sbuf, aown, abuf, cbuf, rel, rbuf, dsend, dbuf, lsend, lbuf,
    ow, dw, ps, bs, pd, st_ref,
    qs, qr, ks, kr, vs, vr, ss, sr, as_, ar, cs, relr, fs, cr, ds_, dr, ls, lr, loc, hello,
):
    S, T, H, rows, local = sizes
    G = S // H
    CP = S // T
    cols = ow.shape[1]
    me = lax.axis_index("seq")
    z = lax.axis_index("tp")
    head = me // G
    g = lax.rem(me, G)

    loads = [
        pltpu.make_async_copy(src, dst, loc.at[n])
        for n, (src, dst) in enumerate(
            ((ow_hbm, ow), (ps_hbm, ps), (dw_hbm, dw), (bs_hbm, bs))
        )
    ]
    for load in loads:
        load.start()

    first = pltpu.make_async_copy(st_hbm, st_ref, loc.at[4])
    first.start()
    barrier = pltpu.get_barrier_semaphore()
    for i in range(1, S):
        pl.semaphore_signal(
            barrier, inc=1, device_id={"seq": lax.rem(me + i, S), "tp": z}, device_id_type=MESH
        )

    def greet(sem):
        @pl.when(z > 0)
        def _():
            pl.semaphore_signal(
                sem, inc=1, device_id={"seq": me, "tp": z - 1}, device_id_type=MESH
            )

        @pl.when(z < T - 1)
        def _():
            pl.semaphore_signal(
                sem, inc=1, device_id={"seq": me, "tp": z + 1}, device_id_type=MESH
            )

    beside = jnp.where(z > 0, 1, 0) + jnp.where(z < T - 1, 1, 0)
    greet(barrier)
    first.wait()
    starts = jnp.broadcast_to(st_ref[...], (8, rows))
    valid8 = jnp.where(starts < B_DEV, 1.0, 0.0)
    sbuf[me] = valid8

    pl.semaphore_wait(barrier, S - 1 + beside)
    if T > 2:
        greet(hello.at[0])

    def lanes(block, width):
        return pl.ds(pl.multiple_of(block * width, 128), width)

    sends = []

    def send(src, dst, ssem, rsem, seq, tp):
        copy = pltpu.make_async_remote_copy(
            src_ref=src, dst_ref=dst, send_sem=ssem, recv_sem=rsem,
            device_id={"seq": seq, "tp": tp}, device_id_type=MESH,
        )
        copy.start()
        sends.append(copy)

    def arrived(dst, sem):
        pltpu.make_async_copy(dst, dst, sem).wait()

    for i in range(S):
        tgt = lax.rem(me + i, S)
        part = lanes(tgt // G, DH)
        if i == 0:
            pltpu.make_async_copy(k_hbm.at[:, part], kbuf.at[me], kr.at[me]).start()
            pltpu.make_async_copy(v_hbm.at[:, part], vbuf.at[me], vr.at[me]).start()
            pltpu.make_async_copy(q_hbm.at[:, part], qbuf.at[head], qr.at[head]).start()
        else:
            send(k_hbm.at[:, part], kbuf.at[me], ks.at[i], kr.at[me], tgt, z)
            if i % G == 0:
                send(q_hbm.at[:, part], qbuf.at[head], qs.at[i], qr.at[head], tgt, z)
            send(sbuf.at[me], sbuf.at[me], ss.at[i], sr.at[me], tgt, z)
            send(v_hbm.at[:, part], vbuf.at[me], vs.at[i], vr.at[me], tgt, z)

    count = S * rows
    key_row = lax.broadcasted_iota(jnp.int32, (rows, count), 1)
    slot = lax.broadcasted_iota(jnp.int32, (rows, count), 0)
    spread = key_row == slot
    for d in range(1, S):
        spread = spread | (key_row == slot + d * rows)
    spread = jnp.where(spread, 1.0, 0.0).astype(jnp.bfloat16)

    for i in range(1, S):
        src = lax.rem(me + i, S)
        arrived(sbuf.at[src], sr.at[src])
    which = lax.broadcasted_iota(jnp.int32, (S, rows), 0)
    valid = jnp.zeros((S, rows), jnp.float32)
    for d in range(S):
        valid = jnp.where(which == d, sbuf[d][:1, :], valid)
    laid = jnp.dot(valid.astype(jnp.bfloat16), spread, preferred_element_type=jnp.float32)
    owner = lax.broadcasted_iota(jnp.int32, (S, count), 0) * rows
    lane = lax.broadcasted_iota(jnp.int32, (S, count), 1)
    laid = jnp.where((lane >= owner) & (lane < owner + rows), laid, 0.0)
    key_valid = jnp.sum(laid, axis=0, keepdims=True)

    mine = H * rows
    row = lax.broadcasted_iota(jnp.int32, (mine, count), 0)
    block = jnp.zeros((mine, count), jnp.int32)
    for j in range(1, H):
        block = block + jnp.where(row >= j * rows, (G - 1) * rows, 0)
    query = row + block + g * rows
    key = lax.broadcasted_iota(jnp.int32, (mine, count), 1)
    allowed = (key <= query) & (key_valid > 0.0)

    for j in range(H):
        arrived(qbuf.at[j], qr.at[j])
    for d in range(S):
        arrived(kbuf.at[d], kr.at[d])
    scores = lax.dot_general(
        qbuf[...].reshape(mine, DH), kbuf[...].reshape(count, DH),
        (((1,), (1,)), ((), ())), preferred_element_type=jnp.float32,
    ) * (DH ** -0.5)
    scores = jnp.where(allowed, scores, NEG)
    peak = jnp.max(scores, axis=1, keepdims=True)
    expo = jnp.exp(scores - peak)
    total = jnp.sum(expo, axis=1, keepdims=True)
    for d in range(S):
        arrived(vbuf.at[d], vr.at[d])
    summed = jnp.dot(
        expo.astype(jnp.bfloat16), vbuf[...].reshape(count, DH),
        preferred_element_type=jnp.float32,
    )
    aown[...] = (summed / total).astype(jnp.bfloat16).reshape(H, rows, DH)

    own = abuf.at[g, :, :, lanes(head, DH)]
    pltpu.make_async_copy(aown, own, ar.at[me]).start()
    for jj in range(1, H):
        tgt = lax.rem(head + jj, H) * G + g
        send(aown, own, as_.at[jj * G], ar.at[me], tgt, z)
    for e in range(1, G):
        send(aown, own, as_.at[e], ar.at[me], head * G + lax.rem(g + e, G), z)
    for n in range(1, T - 2):
        pl.semaphore_wait(hello.at[n - 1], beside)
        greet(hello.at[n])
    loads[0].wait()

    for e in range(G):
        gg = lax.rem(g + e, G)
        for jj in range(H):
            h = lax.rem(head - jj + H, H)
            src = h * G + gg
            arrived(aown, ar.at[src])
            if e == 0 and jj > 0:
                piece = abuf.at[g, :, :, lanes(h, DH)]
                for f in range(1, G):
                    partner = head * G + lax.rem(g + f, G)
                    send(piece, piece, as_.at[jj * G + f], ar.at[src], partner, z)
        product = jnp.dot(
            abuf[gg].reshape(mine, H * DH), ow[...], preferred_element_type=jnp.float32
        )
        cbuf[gg] = product.astype(jnp.bfloat16).reshape(H, rows, cols)
        for jj in range(H):
            j = lax.rem(head + jj, H)
            tgt = j * G + gg
            if e == 0 and jj == 0:
                pltpu.make_async_copy(cbuf.at[gg, j], rel.at[me], relr.at[me]).start()
            else:
                send(cbuf.at[gg, j], rel.at[me], cs.at[e * H + jj], relr.at[me], tgt, z)

    if T > 2:
        pl.semaphore_wait(hello.at[T - 3], beside)
    passed = []
    for e in range(G):
        for jj in range(H):
            src = lax.rem(head - jj + H, H) * G + lax.rem(g - e + G, G)
            chunk, place = src // CP, lax.rem(src, CP)
            arrived(rel.at[src], relr.at[src])
            dst, dsem = rbuf.at[z, place], cr.at[z, place]
            onward = pltpu.make_async_remote_copy(
                src_ref=rel.at[src], dst_ref=dst, send_sem=fs.at[e * H + jj], recv_sem=dsem,
                device_id={"seq": me, "tp": chunk}, device_id_type=MESH,
            )
            away = chunk != z
            pl.when(away)(onward.start)

            @pl.when(jnp.logical_not(away))
            def _():
                pltpu.make_async_copy(rel.at[src], dst, dsem).start()

            passed.append((away, onward))

    loads[1].wait()
    loads[2].wait()
    wide = dw.shape[1]
    padded = dbuf.shape[2]
    down = jnp.zeros((rows, wide), jnp.float32)
    for n in range(CP):
        p = lax.rem(g + n, CP)
        for t in range(T):
            arrived(rbuf.at[t, p], cr.at[t, p])
        mixed = rbuf[0, p].astype(jnp.float32)
        for t in range(1, T):
            mixed = mixed + rbuf[t, p].astype(jnp.float32)
        at = lanes(p, cols)
        patches = (ps[:, at].astype(jnp.float32) + mixed).astype(jnp.bfloat16)
        np_out[:, at] = patches
        down = down + jnp.dot(patches, dw[at, :], preferred_element_type=jnp.float32)

    def turned(x, t):
        return (x if t == 0 else pltpu.roll(x, wide - t * local, 1))[:, :padded]

    for t in range(T):
        dsend[t] = turned(down, t).astype(jnp.bfloat16)
    for i in range(1, T):
        t = lax.rem(z + i, T)
        send(dsend.at[t], dbuf.at[z], ds_.at[i], dr.at[z], me, t)
    dbuf[z] = dsend[z]

    held = jnp.sum(valid8[:1, :], axis=1, keepdims=True)
    lane16 = lax.broadcasted_iota(jnp.int32, (16, rows), 1).astype(jnp.float32)
    pick = jnp.where(lane16 == held - 1.0, 1.0, 0.0).astype(jnp.bfloat16)
    last = jnp.dot(pick, down.astype(jnp.bfloat16), preferred_element_type=jnp.float32)
    for t in range(T):
        lsend[t] = turned(last, t)[:1, :]
    after = lax.rem(me + 1, S)
    for i in range(T):
        t = lax.rem(z + i, T)
        send(lsend.at[t], lbuf.at[z], ls.at[i], lr.at[z], after, t)

    position = lax.broadcasted_iota(jnp.int32, (B_DEV, rows), 0)
    begun = jnp.where(st_ref[...] <= position, 1.0, 0.0)
    reached = jnp.sum(begun, axis=1, keepdims=True)
    lane_b = lax.broadcasted_iota(jnp.int32, (B_DEV, rows), 1).astype(jnp.float32)
    member = jnp.where(lane_b == reached - 1.0, 1.0, 0.0).astype(jnp.bfloat16)
    before = reached < 0.5
    loads[3].wait()

    for i in range(1, T):
        t = lax.rem(z + i, T)
        arrived(dbuf.at[t], dr.at[t])
    for t in range(T):
        arrived(lbuf.at[t], lr.at[t])
    state = dbuf[0].astype(jnp.float32)
    earlier = lbuf[0]
    for t in range(1, T):
        state = state + dbuf[t].astype(jnp.float32)
        earlier = earlier + lbuf[t]
    state = state.astype(jnp.bfloat16)
    earlier = earlier.astype(jnp.bfloat16).astype(jnp.float32)
    added = jnp.dot(member, state, preferred_element_type=jnp.float32)
    pd[...] = jnp.where(before, earlier, added)
    nb_out[...] = (bs[...].astype(jnp.float32) + pd[:, :local]).astype(jnp.bfloat16)

    for copy in sends:
        copy.wait_send()

    for away, onward in passed:
        pl.when(away)(onward.wait_send)


def put_out(np_ref, nb_ref, np_hbm, nb_hbm, sems):
    copies = [
        pltpu.make_async_copy(np_ref, np_hbm, sems.at[0]),
        pltpu.make_async_copy(nb_ref, nb_hbm, sems.at[1]),
    ]
    for copy in copies:
        copy.start()
    for copy in copies:
        copy.wait()


def fused_form(
    S, T, queries, keys, values, patch_stream, out_weight, down_weight, byte_states, patch_starts
):
    rows, width = queries.shape
    H = width // DH
    G = S // H
    cols = out_weight.shape[1]
    bytes_here, local = byte_states.shape
    padded = -(-local // 128) * 128
    bf = jnp.bfloat16
    sem = pltpu.SemaphoreType.DMA
    scratch = [
        pltpu.VMEM((H, rows, DH), bf),
        pltpu.VMEM((S, rows, DH), bf),
        pltpu.VMEM((S, rows, DH), bf),
        pltpu.VMEM((S, 8, rows), jnp.float32),
        pltpu.VMEM((H, rows, DH), bf),
        pltpu.VMEM((G, H, rows, width), bf),
        pltpu.VMEM((G, H, rows, cols), bf),
        pltpu.VMEM((S, rows, cols), bf),
        pltpu.VMEM((T, S // T, rows, cols), bf),
        pltpu.VMEM((T, rows, padded), bf),
        pltpu.VMEM((T, rows, padded), bf),
        pltpu.VMEM((T, 1, padded), jnp.float32),
        pltpu.VMEM((T, 1, padded), jnp.float32),
        pltpu.VMEM(out_weight.shape, bf),
        pltpu.VMEM(down_weight.shape, bf),
        pltpu.VMEM(patch_stream.shape, bf),
        pltpu.VMEM(byte_states.shape, bf),
        pltpu.VMEM((bytes_here, padded), jnp.float32),
        pltpu.VMEM(patch_starts.shape, jnp.int32),
        sem((S,)), sem((H,)), sem((S,)), sem((S,)), sem((S,)), sem((S,)),
        sem((S,)), sem((S,)), sem((S,)), sem((S,)), sem((S,)), sem((S,)), sem((S,)),
        sem((T, S // T)),
        sem((T,)), sem((T,)), sem((T,)), sem((T,)), sem((5,)),
        pltpu.SemaphoreType.REGULAR((max(T - 2, 1),)),
    ]
    hbm = pl.BlockSpec(memory_space=pltpu.HBM)
    vmem = pl.BlockSpec(memory_space=pltpu.VMEM)
    held = pl.pallas_call(
        functools.partial(fused_kernel, (S, T, H, rows, local)),
        out_shape=(
            jax.ShapeDtypeStruct(patch_stream.shape, bf),
            jax.ShapeDtypeStruct(byte_states.shape, bf),
        ),
        in_specs=[hbm] * 8,
        out_specs=(vmem, vmem),
        scratch_shapes=scratch,
        compiler_params=pltpu.CompilerParams(collective_id=0, has_side_effects=True, vmem_limit_bytes=24 << 20),
    )(*(
        pltpu.with_memory_space_constraint(x, pltpu.HBM)
        for x in (
            queries, keys, values, patch_stream,
            out_weight, down_weight, byte_states, patch_starts,
        )
    ))
    return tuple(pl.pallas_call(
        put_out,
        out_shape=(
            jax.ShapeDtypeStruct(patch_stream.shape, bf),
            jax.ShapeDtypeStruct(byte_states.shape, bf),
        ),
        in_specs=[vmem, vmem],
        out_specs=(hbm, hbm),
        scratch_shapes=[sem((2,))],
        compiler_params=pltpu.CompilerParams(vmem_limit_bytes=4 << 20),
    )(*held))


def on_device(S, T, *args):
    queries, out_weight = args[0], args[4]
    heads = queries.shape[1] // DH
    aligned = out_weight.shape[1] % 128 == 0 and queries.shape[0] % 16 == 0
    if aligned and S % heads == 0 and S % T == 0 and S >= T:
        return fused_form(S, T, *args)
    return plain_form(*args)


def solution(mesh):
    in_specs = (
        P("seq", "tp"),
        P("seq", "tp"),
        P("seq", "tp"),
        P("seq", "tp"),
        P("tp", "seq"),
        P("tp", None),
        P("seq", "tp"),
        P("seq", None),
    )
    out_specs = (P("seq", "tp"), P("seq", "tp"))
    return jax.shard_map(
        functools.partial(on_device, mesh.shape["seq"], mesh.shape["tp"]),
        mesh=mesh, in_specs=in_specs, out_specs=out_specs, check_vma=False
    )
```
